128 devices in a mesh: group: 8 (over x, core), member: 16 (over z, y).
Axes of the slice: x: 4, y: 4, z: 4, core: 2. Of those that a mesh axis runs over, the one named last changes fastest.
Arguments:
- velocity: bfloat16 [32768, 3, 512], P(('group', 'member')), may hold values from -6 to 6
- elem_scale: float32 [32768, 3], P(('group', 'member')), may hold values from 0.05 to 0.4
- face_map: int32 [32768, 64], P(('group', 'member')), may hold values from 0 to 63, each once within a row
- ref_coords: float32 [3, 131072], P(None, ('group', 'member')), may hold values from -1 to 1
- owner_dev: int32 [131072, 1], P(('group', 'member')), may hold values from 0 to 127; in each aligned block of 1024 rows (0 to 1023, 1024 to 2047, ...) at most 16 rows name the same one
- owner_elem: int32 [131072], P(('group', 'member')), may hold values from 0 to 255
Outputs:
- grad_mean: bfloat16 [32768, 9, 512], P(('group', 'member'))
- particle_values: float32 [12, 131072], P(None, ('group', 'member'))
The draws below stay inside these ranges and needn't reach their ends.
Inputs may be any that keep to these rules, and one draw needn't show every extreme that they name: `owner_dev`: within the rows of one device no device is named more than 16 times; that bound is reached. `face_map`: each row is a permutation of 0 to 63.
All inputs are finite; a program needn't handle non-finite values.
Results may differ from the reference program's by a relative error of at most 0.0054.
Values sent between devices are 32-bit elements; how exact they have to be, the bound alone decides.
A program may use at most 64 MiB of HBM per device.

```python
import math
import jax
import jax.numpy as jnp
import numpy as np
from jax import lax

NODES = 512
EC = 256
E_DEV = 256
TOTAL_E = 32768
P_DEV = 1024
PARTS_SIZE = 131072
CAP = 16
DEVICES = 128


def place_ends(values, key, smallest, high):
    index_at = [jax.random.randint(jax.random.fold_in(key, axis), (), 0, length) for axis, length in enumerate(values.shape)]
    main_axis = values.shape.index(max(values.shape))
    beside = index_at[:main_axis] + [(index_at[main_axis] + 1) % values.shape[main_axis]] + index_at[main_axis + 1:]
    return values.at[tuple(index_at)].set(smallest).at[tuple(beside)].set(high)


def block_levels(own_key, extent, pieces, least, largest):
    def one(dim, blocks):
        heights = jax.random.uniform(jax.random.fold_in(jax.random.fold_in(own_key, 6), dim), (blocks,), jnp.float32, least / len(pieces), largest / len(pieces))
        return jnp.repeat(jnp.exp(heights), extent[dim] // blocks).reshape((-1,) + (1,) * (len(extent) - dim - 1))

    level = one(*pieces[0])
    for cut in pieces[1:]:
        level = level * one(*cut)
    return level


def assign_block(rng, own, number, rows, count, top, reach, slope):
    sequence = jax.random.permutation(rng, count)
    heavy_load, common = portions_of(count, rows * top, reach, slope, True), portions_of(count, rows * top, reach, slope, False)
    places = jnp.arange(count)

    def named(lengths, rotation):
        used = int((lengths > 0).sum())
        fixed = max(1, used // 4)
        shifted = fixed + (places - fixed + rotation * (used - fixed)) % max(1, count - fixed)
        return jnp.zeros((count,), jnp.int32).at[sequence[jnp.where(places < fixed, places, shifted)]].set(jnp.asarray(lengths, jnp.int32))

    lengths = jnp.where(number % 4 == 0, named(heavy_load, number // 4), named(common, number - number // 4 - 1))
    mixed = jax.random.permutation(jax.random.fold_in(own, 3), count)
    giver, receiver = mixed[0:count // 2 * 2:2], mixed[1:count // 2 * 2:2]
    slack = jnp.minimum(lengths[giver] - 1, reach - lengths[receiver]) // 2
    slack = jnp.where((giver == sequence[0]) | (receiver == sequence[0]) | (lengths[receiver] == 0), 0, jnp.maximum(slack, 0))
    shifted = jax.random.randint(jax.random.fold_in(own, 4), (count // 2,), 0, 1 << 20) % (slack + 1)
    lengths = lengths.at[giver].add(-shifted).at[receiver].add(shifted)
    items = jnp.searchsorted(jnp.cumsum(lengths), jnp.arange(rows * top), side="right").astype(jnp.int32)
    table = items.reshape(top, rows).T
    table = table[jax.random.permutation(jax.random.fold_in(own, 1), rows)]
    rotation = jax.random.randint(jax.random.fold_in(own, 2), (rows, 1), 0, top)
    return jnp.take_along_axis(table, (jnp.arange(top)[None, :] + rotation) % top, axis=1)


def portions_of(amount, total, most, lean, full):
    loads = [(1 << 20) // math.isqrt(grade ** lean) + 1 for grade in range(1, amount + 1)]
    largest = most if full else min(most, max(-(-total // amount), total * loads[0] // sum(loads)))
    least = 1 if total - largest >= amount - 1 else 0
    counts, spare = [largest] + [least] * (amount - 1), total - largest - least * (amount - 1)
    while spare > 0:
        candidates = [i for i in range(1, amount) if counts[i] < largest] or [i for i in range(1, amount) if counts[i] < most]
        pool, remaining = sum([loads[i] for i in candidates]), spare
        for i in candidates:
            more = min(most - counts[i], max(1, remaining * loads[i] // pool), spare)
            counts[i] = counts[i] + more
            spare = spare - more
    return np.array(counts)


def centred(key, shape, width, limit, pieces=(), held_as=jnp.bfloat16):
    values = width * jax.random.normal(key, shape, jnp.float32)
    if pieces:
        values = values * block_levels(key, shape, pieces, -0.22, 0.18)
    return jnp.clip(values, -limit, limit).astype(held_as)


def setup_inputs(seed: int = 0) -> dict:
    seeds = jax.random.split(jax.random.key(seed), 7)
    velocity = centred(seeds[0], (TOTAL_E, 3, NODES), 1.0, 6.0, ((0, 128),))
    elem_scale = jnp.clip(jnp.exp(math.log(0.4) - 2.0794415 * jax.random.uniform(seeds[1], (TOTAL_E, 3), jnp.float32) ** block_levels(seeds[1], (TOTAL_E, 3), ((0, 128),), -0.2, 0.2)), 0.05, 0.4)
    face_map = jax.vmap(lambda own: jax.random.permutation(own, 64))(jax.random.split(seeds[2], TOTAL_E)).reshape((TOTAL_E, 64)).astype(jnp.int32)
    ref_coords = jnp.clip(jax.random.uniform(seeds[3], (3, PARTS_SIZE), jnp.float32, -1.0, 1.0) * block_levels(seeds[3], (3, PARTS_SIZE), ((1, 128),), -0.4, 0.0), -1.0, 1.0)
    owner_dev_keys = jax.random.split(jax.random.fold_in(seeds[4], 1), PARTS_SIZE // P_DEV)
    owner_dev_turns = jax.random.permutation(jax.random.fold_in(seeds[4], 3), PARTS_SIZE // P_DEV)
    owner_dev = jax.vmap(lambda own, number: assign_block(jax.random.fold_in(seeds[4], 2), own, number, P_DEV, DEVICES, 1, CAP, 2))(owner_dev_keys, owner_dev_turns).reshape((PARTS_SIZE, 1))
    owner_elem = place_ends(jax.random.randint(seeds[5], (PARTS_SIZE,), 0, E_DEV), jax.random.fold_in(seeds[5], 1), 0, E_DEV - 1).astype(jnp.int32)
    return {"velocity": velocity, "elem_scale": elem_scale, "face_map": face_map, "ref_coords": ref_coords, "owner_dev": owner_dev, "owner_elem": owner_elem}


def gll_nodes():
    return -np.cos(np.pi * np.arange(8) / 7.0)


def derivative_table():
    nodes = gll_nodes()
    weights = np.array([np.prod([nodes[first] - nodes[other] for other in range(8) if other != first]) for first in range(8)])
    deriv = np.zeros((8, 8))
    for first in range(8):
        for second in range(8):
            if first != second:
                deriv[first, second] = (weights[first] / weights[second]) / (nodes[first] - nodes[second])
            else:
                deriv[first, first] = sum(1.0 / (nodes[first] - nodes[other]) for other in range(8) if other != first)
    ident = np.eye(8)
    trans = deriv.T
    blocks = [np.kron(np.kron(trans, ident), ident), np.kron(np.kron(ident, trans), ident), np.kron(np.kron(ident, ident), trans)]
    return np.concatenate(blocks, axis=1)


def bottom_index():
    return np.array([first * 64 + second * 8 for first in range(8) for second in range(8)], dtype=np.int32)


def lagrange(coordinate):
    nodes = gll_nodes()
    rows = []
    for first in range(8):
        term = jnp.ones_like(coordinate)
        for second in range(8):
            if second != first:
                term = term * ((coordinate - float(nodes[second])) / float(nodes[first] - nodes[second]))
        rows.append(term)
    return jnp.stack(rows, axis=0)


def node_weights(coords):
    along_r = lagrange(coords[0])
    along_s = lagrange(coords[1])
    along_t = lagrange(coords[2])
    table = (along_r[:, None, None, :] * along_s[None, :, None, :]) * along_t[None, None, :, :]
    return table.reshape(512, coords.shape[1])


def interpolate(vel_rows, grad_rows, weights):
    first = jnp.einsum('bcn,nb->cb', vel_rows.astype(jnp.float32), weights, precision=lax.Precision.HIGHEST)
    second = jnp.einsum('bcn,nb->cb', grad_rows.astype(jnp.float32), weights, precision=lax.Precision.HIGHEST)
    return jnp.concatenate([first, second], axis=0)


def reference(velocity, elem_scale, face_map, ref_coords, owner_dev, owner_elem):
    total = velocity.shape[0]
    table_np = derivative_table().astype(np.float32)
    table = jnp.asarray(table_np).astype(jnp.bfloat16)
    low_index = bottom_index()
    high_index = low_index + 7
    face_cols = np.concatenate([direction * 512 + np.concatenate([low_index, high_index]) for direction in range(3)])
    face_table = jnp.asarray(table_np[:, face_cols]).astype(jnp.bfloat16)
    block_count = total // E_DEV
    vel_blocks = velocity.reshape(block_count, E_DEV * 3, 512)
    scale_blocks = elem_scale.reshape(block_count, E_DEV, 3)

    def face_block(args):
        vel_part, scale_part = args
        result = jnp.dot(vel_part, face_table, preferred_element_type=jnp.float32).reshape(E_DEV, 3, 3, 128)
        result = (result * scale_part[:, None, :, None]).reshape(E_DEV, 9, 128)
        return result[:, :, :64], result[:, :, 64:]

    bottom, top_faces = lax.map(face_block, (vel_blocks, scale_blocks))
    bottom = bottom.reshape(total, 9, 64)
    top_faces = top_faces.reshape(total, 9, 64)
    top_prior = jnp.roll(top_faces, EC, axis=0)
    bottom_mean = 0.5 * (bottom + jnp.take_along_axis(top_prior, face_map[:, None, :], axis=2))
    inverse = jnp.argsort(face_map, axis=1).astype(jnp.int32)
    bottom_turned = jnp.take_along_axis(bottom, inverse[:, None, :], axis=2)
    top_mean = 0.5 * (top_faces + jnp.roll(bottom_turned, -EC, axis=0))

    def grad_block(args):
        vel_part, scale_part, low_part, high_part = args
        result = jnp.dot(vel_part, table, preferred_element_type=jnp.float32).reshape(E_DEV, 3, 3, 512)
        result = (result * scale_part[:, None, :, None]).reshape(E_DEV, 9, 512)
        result = result.at[:, :, low_index].set(low_part).at[:, :, high_index].set(high_part)
        return result.astype(jnp.bfloat16)

    grad_mean = lax.map(grad_block, (vel_blocks, scale_blocks, bottom_mean.reshape(block_count, E_DEV, 9, 64), top_mean.reshape(block_count, E_DEV, 9, 64)))
    grad_mean = grad_mean.reshape(total, 9, 512)
    global_elem = (owner_dev[:, 0] * E_DEV + owner_elem).astype(jnp.int32)
    parts = global_elem.shape[0]

    def part_block(args):
        element_ids, coords = args
        return interpolate(velocity[element_ids], grad_mean[element_ids], node_weights(coords))

    values = lax.map(part_block, (global_elem.reshape(-1, P_DEV), ref_coords.reshape(3, -1, P_DEV).transpose(1, 0, 2)))
    particle_values = values.transpose(1, 0, 2).reshape(12, parts)
    return grad_mean, particle_values
```

```python
import functools

import jax
import jax.numpy as jnp
import numpy as np
from jax import lax
from jax.experimental import pallas as pl
from jax.experimental.pallas import tpu as pltpu
from jax.sharding import PartitionSpec as P

MESH = pl.DeviceIdType.MESH
F32, BF16 = jnp.float32, jnp.bfloat16
NDEV, CAP = 128, 16


def gll_nodes():
    return -np.cos(np.pi * np.arange(8) / 7.0)


def deriv_matrix():
    nodes = gll_nodes()
    weights = np.array([np.prod([nodes[a] - nodes[b] for b in range(8) if b != a]) for a in range(8)])
    deriv = np.zeros((8, 8))
    for a in range(8):
        for b in range(8):
            if a != b:
                deriv[a, b] = weights[a] / weights[b] / (nodes[a] - nodes[b])
            else:
                deriv[a, a] = sum(1.0 / (nodes[a] - nodes[o]) for o in range(8) if o != a)
    return deriv


def tables():
    dt = deriv_matrix().astype(np.float32).T
    eye = np.eye(8, dtype=np.float32)
    gr = np.kron(np.kron(dt, eye), eye)
    gs = np.kron(np.kron(eye, dt), eye)
    gt = np.kron(np.kron(eye, eye), dt)
    low = 8 * np.arange(64)
    ident = np.eye(512, dtype=np.float32)
    face = np.concatenate([ident[:, low + 7], gt[:, low + 7], ident[:, low], gt[:, low]], axis=1)
    fr, fs = np.kron(dt, eye), np.kron(eye, dt)
    inner = np.zeros((256, 256), np.float32)
    inner[0:64, 0:64] = fr
    inner[128:192, 64:128] = fr
    inner[0:64, 128:192] = fs
    inner[128:192, 192:256] = fs
    block = np.concatenate([gs[:256, :256], gt[:256, :256]], axis=1)
    upper = np.triu(np.ones((128, 128), np.float32), 1)
    count = np.concatenate([upper, np.ones((128, 128), np.float32)], axis=1)
    return [jnp.asarray(t, BF16) for t in (face, gr, block, inner, count)]


def rounded_deriv():
    return deriv_matrix().astype(np.float32).astype(jnp.dtype(BF16)).astype(np.float32)


def split3(x):
    hi = x.astype(BF16)
    rest = x - hi.astype(F32)
    mid = rest.astype(BF16)
    return hi, mid, (rest - mid.astype(F32)).astype(BF16)


def dot(a, b):
    return jnp.dot(a, b, preferred_element_type=F32)


def dot_t(a, b):
    return lax.dot_general(a, b, (((1,), (1,)), ((), ())), preferred_element_type=F32)


def iota(shape, axis):
    return lax.broadcasted_iota(jnp.int32, shape, axis)


def take_lanes(x, idx):
    return jnp.take_along_axis(x, idx, axis=1, mode="promise_in_bounds")


def column(values):
    row = iota((8, 1), 0)
    out = jnp.full((8, 1), float(values[0]), F32)
    for a in range(1, 8):
        out = jnp.where(row == a, float(values[a]), out)
    return out


def lagrange(y):
    nodes = gll_nodes()
    row = iota(y.shape, 0)
    out = None
    for b in range(8):
        inv = column([1.0 / (nodes[a] - nodes[b]) if a != b else 0.0 for a in range(8)])
        term = jnp.where(row == b, 1.0, (y - float(nodes[b])) * inv)
        out = term if out is None else out * term
    return out


def kernel(v, sc, fm, rc, od, oe, face, gr, block, inner, count, dtab,
           grad, pv,
           topm, botm, rtop, rbot, scp, scn, invs, invr, sreq, rreq, sret, rret,
           scols, vt, hot, zs, zt, res, wts, rj, hot2, sclanes, rt, fmt,
           hs, hr, qs, qr, ps, pr, sem_a, sem_b):
    g, m = lax.axis_index("group"), lax.axis_index("member")
    me = g * 16 + m
    z, y = m // 4, m % 4
    nxt, prv = (me + 1) % NDEV, (me + NDEV - 1) % NDEV
    nxt, prv = (nxt // 16, nxt % 16), (prv // 16, prv % 16)

    bar = pltpu.get_barrier_semaphore()
    partners = [nxt, prv] + [((g + i) % 8, m) for i in range(1, 8)]
    zpart = [(g, ((z + i) % 4) * 4 + y) for i in range(1, 4)]
    ypart = [(g, z * 4 + (y + i) % 4) for i in range(1, 4)]
    for p in partners + zpart + ypart:
        pl.semaphore_signal(bar, inc=1, device_id=p, device_id_type=MESH)

    for c in range(3):
        x = dot(v[c], face[...])
        topm[c] = x[:, :128]
        botm[c] = x[:, 128:]

    fmt[0:64, :] = fm[:, 0:128].astype(F32)
    fmt[64:128, :] = fm[:, 128:256].astype(F32)

    def invert(f, acc):
        lo, hi = acc
        where = iota((64, 128), 0).astype(F32)
        value = f.astype(F32)
        lo = jnp.where(fmt[pl.ds(f, 1), :] == where, value, lo)
        hi = jnp.where(fmt[pl.ds(64 + f, 1), :] == where, value, hi)
        return lo, hi

    zero = jnp.zeros((64, 128), F32)
    inv_lo, inv_hi = lax.fori_loop(0, 64, invert, (zero, zero), unroll=8)
    invs[...] = jnp.concatenate([inv_lo, inv_hi], axis=0).T.astype(jnp.int32)

    running = jnp.zeros((128, 128), F32)
    for b in range(8):
        lanes = slice(128 * b, 128 * b + 128)
        hit = (iota((128, 128), 0) == od[:, lanes]).astype(F32)
        hit16 = hit.astype(BF16)
        hot2[0:128, lanes] = hit16
        hot2[128:256, lanes] = hit16
        before = dot(hit16, count[...])
        rank = jnp.sum(hit * (before[:, :128] + running), axis=0, keepdims=True)
        running = running + before[:, 128:]
        rj[:, lanes] = (iota((16, 128), 0).astype(F32) == rank).astype(F32)
    rows = [rc[i : i + 1, :] for i in range(3)] + [oe[...].astype(F32)]
    spread = jnp.concatenate([rj[...] * row for row in rows] + [jnp.zeros((64, 1024), F32)], axis=0)
    send = None
    for part in split3(spread):
        one = dot_t(hot2[0:128, :], part)
        send = one if send is None else send + one
    sreq[:, 0, :] = send

    pl.semaphore_wait(bar, len(partners) + 6)
    for p in zpart:
        pl.semaphore_signal(sem_a, inc=1, device_id=p, device_id_type=MESH)

    def push(src, dst, k, to):
        copy = pltpu.make_async_remote_copy(
            src_ref=src, dst_ref=dst, send_sem=hs.at[k], recv_sem=hr.at[k], device_id=to, device_id_type=MESH
        )
        copy.start()
        return copy

    halo = [push(sc, scp, 0, nxt), push(sc, scn, 1, prv), push(invs, invr, 2, prv)]
    for c in range(3):
        halo.append(push(topm.at[c], rtop.at[c], 3 + 2 * c, nxt))
        halo.append(push(botm.at[c], rbot.at[c], 4 + 2 * c, prv))

    pl.semaphore_wait(sem_a, 3)
    for p in ypart:
        pl.semaphore_signal(sem_b, inc=1, device_id=p, device_id_type=MESH)
    pl.semaphore_wait(sem_b, 3)

    def exchange(src, dst, ssem, rsem):
        pltpu.make_async_copy(src.at[me], dst.at[me], rsem).start()

        def one(i, carry):
            t = (me + i) % NDEV
            pltpu.make_async_remote_copy(
                src_ref=src.at[t], dst_ref=dst.at[me], send_sem=ssem, recv_sem=rsem,
                device_id=(t // 16, t % 16), device_id_type=MESH,
            ).start()
            return carry

        lax.fori_loop(1, NDEV, one, 0)

    exchange(sreq, rreq, qs, qr)

    for c in range(3):
        vt[c] = v[c].astype(F32).T.astype(BF16)
    for d in range(3):
        for i, part in enumerate(split3(sc[d : d + 1, :])):
            sclanes[3 * d + i : 3 * d + i + 1, :] = part.astype(F32)
    scales16 = jnp.concatenate([sclanes[0:9, :], jnp.zeros((7, 256), F32)], axis=0).astype(BF16)

    pltpu.make_async_copy(rreq, rreq, qr).wait()
    rt[...] = rreq[:, 0, :].T

    half = column([0.5] + [1.0] * 6 + [0.5])
    dr = [dtab[:, 128 * a : 128 * a + 1] for a in range(8)]

    def pair(row, j):
        return jnp.concatenate([rt[pl.ds(row + 2 * j, 1), :], rt[pl.ds(row + 2 * j + 1, 1), :]], axis=1)

    def put(cc, j, val, add):
        for h in range(2):
            part = val[:, 128 * h : 128 * h + 128]
            row = pl.ds(cc * 16 + 2 * j + h, 1)
            res[row, :] = res[row, :] + part if add else part

    def own(j, carry):
        lanes = pl.ds(pl.multiple_of(j * 256, 256), 256)
        lag, der = [], []
        for a in range(3):
            base = lagrange(jnp.broadcast_to(pair(16 * a, j), (8, 256)))
            wts[8 * a : 8 * a + 8, lanes] = base
            lag.append(base)
            use = base * half if a == 2 else base
            total = None
            for b in range(8):
                term = use[b : b + 1, :] * dr[b]
                total = term if total is None else total + term
            der.append(total)
        hit = (iota((256, 256), 0).astype(F32) == pair(48, j)).astype(F32).astype(BF16)
        hot[:, lanes] = hit
        pieces = dot(scales16, hit)
        ht = lag[2] * half
        for c in range(3):
            picked = dot(vt[c], hit)
            s0 = s1 = s2 = jnp.zeros((8, 256), F32)
            for jj in range(8):
                a0 = a1 = jnp.zeros((8, 256), F32)
                for i in range(8):
                    x = picked[64 * i + 8 * jj : 64 * i + 8 * jj + 8, :]
                    a0 = a0 + lag[0][i : i + 1, :] * x
                    a1 = a1 + der[0][i : i + 1, :] * x
                s0 = s0 + lag[1][jj : jj + 1, :] * a0
                s1 = s1 + der[1][jj : jj + 1, :] * a0
                s2 = s2 + lag[1][jj : jj + 1, :] * a1
            put(c, j, jnp.sum(lag[2] * s0, axis=0, keepdims=True), False)
            for d, part in enumerate((ht * s2, ht * s1, der[2] * s0)):
                scale = pieces[3 * d : 3 * d + 1] + pieces[3 * d + 1 : 3 * d + 2] + pieces[3 * d + 2 : 3 * d + 3]
                put(3 + 3 * c + d, j, jnp.sum(part, axis=0, keepdims=True) * scale, False)
        return carry

    lax.fori_loop(0, 8, own, 0)

    for k in range(3):
        halo[k].wait_recv()
    scols[...] = jnp.zeros((128, 128), F32)
    for h in range(2):
        lanes = slice(128 * h, 128 * h + 128)
        scols[8 * h : 8 * h + 3, :] = scp[:, lanes]
        scols[16 + 8 * h : 16 + 8 * h + 3, :] = scn[:, lanes]
        scols[32 + 8 * h : 32 + 8 * h + 3, :] = sc[:, lanes]
    cols = scols[...].T

    def scale_col(base, d):
        first = cols[:, base + d : base + d + 1]
        second = cols[:, base + 8 + d : base + 8 + d + 1]
        return jnp.concatenate([jnp.broadcast_to(first, (128, 128)), jnp.broadcast_to(second, (128, 128))], axis=0)

    left = iota((256, 128), 1) < 64
    both = [jnp.where(left, scale_col(0, d), scale_col(16, d)) for d in range(3)]
    fm2, inv2 = fmt[...].T.astype(jnp.int32), invr[...]
    left2 = iota((128, 128), 1) < 64
    idx = jnp.concatenate(
        [
            jnp.where(left2, fm2, 64 + pltpu.roll(inv2, 64, 1)),
            jnp.where(left2, pltpu.roll(fm2, 64, 1), 64 + inv2),
        ],
        axis=0,
    )

    for c in range(3):
        halo[3 + 2 * c].wait_recv()
        halo[4 + 2 * c].wait_recv()
        up, down = rtop[c], rbot[c]
        rs = dot(jnp.concatenate([up, down], axis=1).astype(BF16), inner[...])
        fields = [rs[:, :128], rs[:, 128:], jnp.where(left, pltpu.roll(up, 64, 1), down)]
        for d in range(3):
            turned = take_lanes(fields[d] * both[d], idx)
            zs[3 * c + d] = turned
            zt[128 * d : 128 * d + 128, :] = turned.T.astype(BF16)

        def neighbours(j, carry):
            lanes = pl.ds(pl.multiple_of(j * 256, 256), 256)
            picked = dot(zt[...], hot[:, lanes])
            lr, ls, lt = wts[0:8, lanes], wts[8:16, lanes], wts[16:24, lanes]
            for d in range(3):
                lo = hi = jnp.zeros((8, 256), F32)
                for i in range(8):
                    at = 128 * d + 8 * i
                    lo = lo + lr[i : i + 1, :] * picked[at : at + 8, :]
                    hi = hi + lr[i : i + 1, :] * picked[at + 64 : at + 72, :]
                both_faces = 0.5 * (lt[0:1, :] * lo + lt[7:8, :] * hi)
                put(3 + 3 * c + d, j, jnp.sum(ls * both_faces, axis=0, keepdims=True), True)
            return carry

        lax.fori_loop(0, 8, neighbours, 0)

    res[192:256, :] = jnp.zeros((64, 128), F32)
    sret[:, 0, :] = res[0:128, :].T
    sret[:, 1, :] = res[128:256, :].T
    exchange(sret, rret, ps, pr)

    spot = iota((256, 128), 1)
    on_face = (spot % 8 == 0) | (spot % 8 == 7)
    source = spot // 8 + jnp.where(spot % 8 == 7, 64, 0)
    for c in range(3):
        full = [dot(v[c], gr[...])]
        halves = [dot(v[c, :, 256 * h : 256 * h + 256], block[...]) for h in range(2)]
        for d in range(3):
            scale = scale_col(32, d)
            near = zs[3 * c + d]
            for t in range(4):
                lanes = slice(128 * t, 128 * t + 128)
                if d == 0:
                    raw = full[0][:, lanes]
                else:
                    at = 256 * (d - 1) + 128 * (t % 2)
                    raw = halves[t // 2][:, at : at + 128]
                raw = raw * scale
                mean = 0.5 * (raw + take_lanes(near, source + 16 * t))
                grad[3 * c + d, :, lanes] = jnp.where(on_face, mean, raw).astype(BF16)

    pltpu.make_async_copy(rret, rret, pr).wait()
    back = jnp.concatenate([rret[:, 0, :].T, rret[:, 1, :].T[0:64, :]], axis=0)
    hi, lo, _ = split3(back)
    rows = dot(jnp.concatenate([hi, lo], axis=1), hot2[...])
    for cc in range(12):
        pv[cc : cc + 1, :] = jnp.sum(rj[...] * rows[16 * cc : 16 * cc + 16, :], axis=0, keepdims=True)

    for copy in halo:
        copy.wait_send()
    for src, sem in ((sreq, qs), (sret, ps)):
        sent = src.at[pl.ds(0, NDEV - 1)]
        pltpu.make_async_copy(sent, sent, sem).wait()


def per_device(velocity, elem_scale, face_map, ref_coords, owner_dev, owner_elem):
    deriv = rounded_deriv()
    dtab = np.repeat(deriv.T, 128, axis=1).astype(np.float32)
    vmem = pl.BlockSpec(memory_space=pltpu.VMEM)
    out = pl.pallas_call(
        kernel,
        out_shape=(
            jax.ShapeDtypeStruct((9, 256, 512), BF16),
            jax.ShapeDtypeStruct((12, 1024), F32),
        ),
        in_specs=[vmem] * 12,
        out_specs=(vmem, vmem),
        scratch_shapes=[
            pltpu.VMEM((3, 256, 128), F32),
            pltpu.VMEM((3, 256, 128), F32),
            pltpu.VMEM((3, 256, 128), F32),
            pltpu.VMEM((3, 256, 128), F32),
            pltpu.VMEM((3, 256), F32),
            pltpu.VMEM((3, 256), F32),
            pltpu.VMEM((128, 128), jnp.int32),
            pltpu.VMEM((128, 128), jnp.int32),
            pltpu.VMEM((128, 1, 128), F32),
            pltpu.VMEM((128, 1, 128), F32),
            pltpu.VMEM((128, 2, 128), F32),
            pltpu.VMEM((128, 2, 128), F32),
            pltpu.VMEM((128, 128), F32),
            pltpu.VMEM((3, 512, 256), BF16),
            pltpu.VMEM((256, 2048), BF16),
            pltpu.VMEM((9, 256, 128), F32),
            pltpu.VMEM((384, 256), BF16),
            pltpu.VMEM((256, 128), F32),
            pltpu.VMEM((24, 2048), F32),
            pltpu.VMEM((16, 1024), F32),
            pltpu.VMEM((256, 1024), BF16),
            pltpu.VMEM((16, 256), F32),
            pltpu.VMEM((128, 128), F32),
            pltpu.VMEM((128, 128), F32),
            pltpu.SemaphoreType.DMA((9,)),
            pltpu.SemaphoreType.DMA((9,)),
            pltpu.SemaphoreType.DMA,
            pltpu.SemaphoreType.DMA,
            pltpu.SemaphoreType.DMA,
            pltpu.SemaphoreType.DMA,
            pltpu.SemaphoreType.REGULAR,
            pltpu.SemaphoreType.REGULAR,
        ],
        compiler_params=pltpu.CompilerParams(
            collective_id=0, has_side_effects=True, vmem_limit_bytes=56 * 1024 * 1024
        ),
    )(
        velocity.transpose(1, 0, 2),
        elem_scale.T,
        face_map.T,
        ref_coords,
        owner_dev.reshape(1, 1024),
        owner_elem.reshape(1, 1024),
        *tables(),
        jnp.asarray(dtab),
    )
    return out[0].transpose(1, 0, 2), out[1]


def solution(mesh):
    both = ("group", "member")
    in_specs = (P(both, None, None), P(both, None), P(both, None), P(None, both), P(both, None), P(both))
    out_specs = (P(both, None, None), P(None, both))
    return jax.shard_map(per_device, mesh=mesh, in_specs=in_specs, out_specs=out_specs, check_vma=False)
```

```python
import functools

import jax
import jax.numpy as jnp
import numpy as np
from jax import lax
from jax.experimental import pallas as pl
from jax.experimental.pallas import tpu as pltpu
from jax.sharding import PartitionSpec as P

MESH = pl.DeviceIdType.MESH
F32, BF16 = jnp.float32, jnp.bfloat16
NDEV, CAP = 128, 16


def gll_nodes():
    return -np.cos(np.pi * np.arange(8) / 7.0)


def deriv_matrix():
    nodes = gll_nodes()
    weights = np.array([np.prod([nodes[a] - nodes[b] for b in range(8) if b != a]) for a in range(8)])
    deriv = np.zeros((8, 8))
    for a in range(8):
        for b in range(8):
            if a != b:
                deriv[a, b] = weights[a] / weights[b] / (nodes[a] - nodes[b])
            else:
                deriv[a, a] = sum(1.0 / (nodes[a] - nodes[o]) for o in range(8) if o != a)
    return deriv


def tables():
    dt = deriv_matrix().astype(np.float32).T
    eye = np.eye(8, dtype=np.float32)
    gr = np.kron(np.kron(dt, eye), eye)
    gs = np.kron(np.kron(eye, dt), eye)
    gt = np.kron(np.kron(eye, eye), dt)
    low = 8 * np.arange(64)
    ident = np.eye(512, dtype=np.float32)
    face = np.concatenate([ident[:, low + 7], gt[:, low + 7], ident[:, low], gt[:, low]], axis=1)
    fr, fs = np.kron(dt, eye), np.kron(eye, dt)
    inner = np.zeros((256, 256), np.float32)
    inner[0:64, 0:64] = fr
    inner[128:192, 64:128] = fr
    inner[0:64, 128:192] = fs
    inner[128:192, 192:256] = fs
    block = np.concatenate([gs[:256, :256], gt[:256, :256]], axis=1)
    upper = np.triu(np.ones((128, 128), np.float32), 1)
    count = np.concatenate([upper, np.ones((128, 128), np.float32)], axis=1)
    return [jnp.asarray(t, BF16) for t in (face, gr, block, inner, count)]


def rounded_deriv():
    return deriv_matrix().astype(np.float32).astype(jnp.dtype(BF16)).astype(np.float32)


def split3(x):
    hi = x.astype(BF16)
    rest = x - hi.astype(F32)
    mid = rest.astype(BF16)
    return hi, mid, (rest - mid.astype(F32)).astype(BF16)


def dot(a, b):
    return jnp.dot(a, b, preferred_element_type=F32)


def dot_t(a, b):
    return lax.dot_general(a, b, (((1,), (1,)), ((), ())), preferred_element_type=F32)


def iota(shape, axis):
    return lax.broadcasted_iota(jnp.int32, shape, axis)


def take_lanes(x, idx):
    return jnp.take_along_axis(x, idx, axis=1, mode="promise_in_bounds")


def column(values):
    row = iota((8, 1), 0)
    out = jnp.full((8, 1), float(values[0]), F32)
    for a in range(1, 8):
        out = jnp.where(row == a, float(values[a]), out)
    return out


def lagrange(y):
    nodes = gll_nodes()
    row = iota(y.shape, 0)
    out = None
    for b in range(8):
        inv = column([1.0 / (nodes[a] - nodes[b]) if a != b else 0.0 for a in range(8)])
        term = jnp.where(row == b, 1.0, (y - float(nodes[b])) * inv)
        out = term if out is None else out * term
    return out


def far_first():
    hops = [0, 1, 2, 1]
    every = [(x, y, z, c) for x in range(4) for y in range(4) for z in range(4) for c in range(2)]
    every.remove((0, 0, 0, 0))
    return sorted(every, key=lambda o: -(hops[o[0]] + hops[o[1]] + hops[o[2]]))


def kernel(v_in, sc_in, fm_in, rc_in, od_in, oe_in, face_in, gr_in, block_in, inner_in, count_in, dtab_in,
           grad, pv,
           v, sc, fm, rc, od, oe, face, gr, block, inner, count, dtab,
           topm, botm, rtop, rbot, scp, scn, invs, invr, sreq, rreq, sret, rret,
           scols, vt, hot, zs, zt, res, wts, rj, hot2, sclanes, rt, fmt,
           ins, hs, hr, qs, qr, ps, pr, sem_a, sem_b):
    loads = {}
    order = [("face", face_in, face), ("v0", v_in.at[0], v.at[0]), ("v1", v_in.at[1], v.at[1]),
             ("v2", v_in.at[2], v.at[2]), ("sc", sc_in, sc), ("od", od_in, od), ("count", count_in, count),
             ("rc", rc_in, rc), ("oe", oe_in, oe), ("fm", fm_in, fm), ("inner", inner_in, inner),
             ("dtab", dtab_in, dtab), ("gr", gr_in, gr), ("block", block_in, block)]
    for k, (name, src, dst) in enumerate(order):
        loads[name] = pltpu.make_async_copy(src, dst, ins.at[k])
        loads[name].start()

    g, m = lax.axis_index("group"), lax.axis_index("member")
    me = g * 16 + m
    core, x, z, y = g % 2, g // 2, m // 4, m % 4
    nxt, prv = (me + 1) % NDEV, (me + NDEV - 1) % NDEV
    nxt, prv = (nxt // 16, nxt % 16), (prv // 16, prv % 16)

    bar = pltpu.get_barrier_semaphore()
    partners = [nxt, prv] + [((g + i) % 8, m) for i in range(1, 8)]
    zpart = [(g, ((z + i) % 4) * 4 + y) for i in range(1, 4)]
    ypart = [(g, z * 4 + (y + i) % 4) for i in range(1, 4)]
    for p in partners + zpart + ypart:
        pl.semaphore_signal(bar, inc=1, device_id=p, device_id_type=MESH)

    loads["face"].wait()
    for c in range(3):
        loads["v%d" % c].wait()
        out = dot(v[c], face[...])
        topm[c] = out[:, :128]
        botm[c] = out[:, 128:]
    loads["sc"].wait()

    pl.semaphore_wait(bar, len(partners) + 6)
    for p in zpart:
        pl.semaphore_signal(sem_a, inc=1, device_id=p, device_id_type=MESH)

    def push(src, dst, k, to):
        copy = pltpu.make_async_remote_copy(
            src_ref=src, dst_ref=dst, send_sem=hs.at[k], recv_sem=hr.at[k], device_id=to, device_id_type=MESH
        )
        copy.start()
        return copy

    halo = [push(sc, scp, 0, nxt), push(sc, scn, 1, prv)]
    for c in range(3):
        halo.append(push(topm.at[c], rtop.at[c], 2 + 2 * c, nxt))
        halo.append(push(botm.at[c], rbot.at[c], 3 + 2 * c, prv))
        if c == 0:
            loads["fm"].wait()
            fmt[0:64, :] = fm[:, 0:128].astype(F32)
            fmt[64:128, :] = fm[:, 128:256].astype(F32)

            def invert(f, acc):
                lo, hi = acc
                where = iota((64, 128), 0).astype(F32)
                value = f.astype(F32)
                lo = jnp.where(fmt[pl.ds(f, 1), :] == where, value, lo)
                hi = jnp.where(fmt[pl.ds(64 + f, 1), :] == where, value, hi)
                return lo, hi

            zero = jnp.zeros((64, 128), F32)
            inv_lo, inv_hi = lax.fori_loop(0, 64, invert, (zero, zero), unroll=8)
            invs[...] = jnp.concatenate([inv_lo, inv_hi], axis=0).T.astype(jnp.int32)
            last = push(invs, invr, 8, prv)
    halo.append(last)

    pl.semaphore_wait(sem_a, 3)
    for p in ypart:
        pl.semaphore_signal(sem_b, inc=1, device_id=p, device_id_type=MESH)

    for name in ("od", "count", "rc", "oe"):
        loads[name].wait()
    running = jnp.zeros((128, 128), F32)
    for b in range(8):
        lanes = slice(128 * b, 128 * b + 128)
        hit = (iota((128, 128), 0) == od[:, lanes]).astype(F32)
        hit16 = hit.astype(BF16)
        hot2[0:128, lanes] = hit16
        hot2[128:256, lanes] = hit16
        before = dot(hit16, count[...])
        rank = jnp.sum(hit * (before[:, :128] + running), axis=0, keepdims=True)
        running = running + before[:, 128:]
        rj[:, lanes] = (iota((16, 128), 0).astype(F32) == rank).astype(F32)
    rows = [rc[i : i + 1, :] for i in range(3)] + [oe[...].astype(F32)]
    spread = jnp.concatenate([rj[...] * row for row in rows] + [jnp.zeros((64, 1024), F32)], axis=0)
    send = None
    for part in split3(spread):
        one = dot_t(hot2[0:128, :], part)
        send = one if send is None else send + one
    sreq[:, 0, :] = send

    pl.semaphore_wait(sem_b, 3)

    def exchange(src, dst, ssem, rsem):
        for ox, oy, oz, oc in far_first():
            tg, tm = ((x + ox) % 4) * 2 + (core + oc) % 2, ((z + oz) % 4) * 4 + (y + oy) % 4
            pltpu.make_async_remote_copy(
                src_ref=src.at[tg * 16 + tm], dst_ref=dst.at[me], send_sem=ssem, recv_sem=rsem,
                device_id=(tg, tm), device_id_type=MESH,
            ).start()
        pltpu.make_async_copy(src.at[me], dst.at[me], rsem).start()

    exchange(sreq, rreq, qs, qr)

    for c in range(3):
        vt[c] = v[c].astype(F32).T.astype(BF16)
    for d in range(3):
        for i, part in enumerate(split3(sc[d : d + 1, :])):
            sclanes[3 * d + i : 3 * d + i + 1, :] = part.astype(F32)
    scales16 = jnp.concatenate([sclanes[0:9, :], jnp.zeros((7, 256), F32)], axis=0).astype(BF16)

    for k in (0, 1, 8):
        halo[k].wait_recv()
    scols[...] = jnp.zeros((128, 128), F32)
    for h in range(2):
        lanes = slice(128 * h, 128 * h + 128)
        scols[8 * h : 8 * h + 3, :] = scp[:, lanes]
        scols[16 + 8 * h : 16 + 8 * h + 3, :] = scn[:, lanes]
        scols[32 + 8 * h : 32 + 8 * h + 3, :] = sc[:, lanes]
    cols = scols[...].T

    def scale_col(base, d):
        first = cols[:, base + d : base + d + 1]
        second = cols[:, base + 8 + d : base + 8 + d + 1]
        return jnp.concatenate([jnp.broadcast_to(first, (128, 128)), jnp.broadcast_to(second, (128, 128))], axis=0)

    left = iota((256, 128), 1) < 64
    both = [jnp.where(left, scale_col(0, d), scale_col(16, d)) for d in range(3)]
    fm2, inv2 = fmt[...].T.astype(jnp.int32), invr[...]
    left2 = iota((128, 128), 1) < 64
    idx = jnp.concatenate(
        [
            jnp.where(left2, fm2, 64 + pltpu.roll(inv2, 64, 1)),
            jnp.where(left2, pltpu.roll(fm2, 64, 1), 64 + inv2),
        ],
        axis=0,
    )
    loads["inner"].wait()
    loads["dtab"].wait()

    def build(c):
        halo[2 + 2 * c].wait_recv()
        halo[3 + 2 * c].wait_recv()
        up, down = rtop[c], rbot[c]
        rs = dot(jnp.concatenate([up, down], axis=1).astype(BF16), inner[...])
        fields = [rs[:, :128], rs[:, 128:], jnp.where(left, pltpu.roll(up, 64, 1), down)]
        for d in range(3):
            turned = take_lanes(fields[d] * both[d], idx)
            zs[3 * c + d] = turned
            zt[384 * c + 128 * d : 384 * c + 128 * d + 128, :] = turned.T.astype(BF16)

    build(0)

    pltpu.make_async_copy(rreq, rreq, qr).wait()
    rt[...] = rreq[:, 0, :].T

    half = column([0.5] + [1.0] * 6 + [0.5])
    dr = [dtab[:, 128 * a : 128 * a + 1] for a in range(8)]

    def pair(row, j):
        return jnp.concatenate([rt[pl.ds(row + 2 * j, 1), :], rt[pl.ds(row + 2 * j + 1, 1), :]], axis=1)

    def put(cc, j, val, add):
        for h in range(2):
            part = val[:, 128 * h : 128 * h + 128]
            row = pl.ds(cc * 16 + 2 * j + h, 1)
            res[row, :] = res[row, :] + part if add else part

    def own(j, carry):
        lanes = pl.ds(pl.multiple_of(j * 256, 256), 256)
        lag, der = [], []
        for a in range(3):
            base = lagrange(jnp.broadcast_to(pair(16 * a, j), (8, 256)))
            wts[8 * a : 8 * a + 8, lanes] = base
            lag.append(base)
            use = base * half if a == 2 else base
            total = None
            for b in range(8):
                term = use[b : b + 1, :] * dr[b]
                total = term if total is None else total + term
            der.append(total)
        hit = (iota((256, 256), 0).astype(F32) == pair(48, j)).astype(F32).astype(BF16)
        hot[:, lanes] = hit
        pieces = dot(scales16, hit)
        ht = lag[2] * half
        for c in range(3):
            picked = dot(vt[c], hit)
            s0 = s1 = s2 = jnp.zeros((8, 256), F32)
            for jj in range(8):
                a0 = a1 = jnp.zeros((8, 256), F32)
                for i in range(8):
                    node = picked[64 * i + 8 * jj : 64 * i + 8 * jj + 8, :]
                    a0 = a0 + lag[0][i : i + 1, :] * node
                    a1 = a1 + der[0][i : i + 1, :] * node
                s0 = s0 + lag[1][jj : jj + 1, :] * a0
                s1 = s1 + der[1][jj : jj + 1, :] * a0
                s2 = s2 + lag[1][jj : jj + 1, :] * a1
            put(c, j, jnp.sum(lag[2] * s0, axis=0, keepdims=True), False)
            for d, part in enumerate((ht * s2, ht * s1, der[2] * s0)):
                scale = pieces[3 * d : 3 * d + 1] + pieces[3 * d + 1 : 3 * d + 2] + pieces[3 * d + 2 : 3 * d + 3]
                put(3 + 3 * c + d, j, jnp.sum(part, axis=0, keepdims=True) * scale, False)
        return carry

    lax.fori_loop(0, 8, own, 0)

    build(1)
    build(2)

    def neighbours(j, carry):
        lanes = pl.ds(pl.multiple_of(j * 256, 256), 256)
        picked = dot(zt[...], hot[:, lanes])
        lr, ls, lt = wts[0:8, lanes], wts[8:16, lanes], wts[16:24, lanes]
        for cd in range(9):
            lo = hi = jnp.zeros((8, 256), F32)
            for i in range(8):
                at = 128 * cd + 8 * i
                lo = lo + lr[i : i + 1, :] * picked[at : at + 8, :]
                hi = hi + lr[i : i + 1, :] * picked[at + 64 : at + 72, :]
            both_faces = 0.5 * (lt[0:1, :] * lo + lt[7:8, :] * hi)
            put(3 + cd, j, jnp.sum(ls * both_faces, axis=0, keepdims=True), True)
        return carry

    lax.fori_loop(0, 8, neighbours, 0)

    res[192:256, :] = jnp.zeros((64, 128), F32)
    sret[:, 0, :] = res[0:128, :].T
    sret[:, 1, :] = res[128:256, :].T
    exchange(sret, rret, ps, pr)

    loads["gr"].wait()
    loads["block"].wait()
    spot = iota((256, 128), 1)
    on_face = (spot % 8 == 0) | (spot % 8 == 7)
    source = spot // 8 + jnp.where(spot % 8 == 7, 64, 0)
    for c in range(3):
        full = [dot(v[c], gr[...])]
        halves = [dot(v[c, :, 256 * h : 256 * h + 256], block[...]) for h in range(2)]
        for d in range(3):
            scale = scale_col(32, d)
            near = zs[3 * c + d]
            for t in range(4):
                lanes = slice(128 * t, 128 * t + 128)
                if d == 0:
                    raw = full[0][:, lanes]
                else:
                    at = 256 * (d - 1) + 128 * (t % 2)
                    raw = halves[t // 2][:, at : at + 128]
                raw = raw * scale
                mean = 0.5 * (raw + take_lanes(near, source + 16 * t))
                grad[3 * c + d, :, lanes] = jnp.where(on_face, mean, raw).astype(BF16)

    pltpu.make_async_copy(rret, rret, pr).wait()
    back = jnp.concatenate([rret[:, 0, :].T, rret[:, 1, :].T[0:64, :]], axis=0)
    hi, lo, _ = split3(back)
    rows = dot(jnp.concatenate([hi, lo], axis=1), hot2[...])
    for cc in range(12):
        pv[cc : cc + 1, :] = jnp.sum(rj[...] * rows[16 * cc : 16 * cc + 16, :], axis=0, keepdims=True)

    for copy in halo:
        copy.wait_send()
    for src, sem in ((sreq, qs), (sret, ps)):
        sent = src.at[pl.ds(0, NDEV - 1)]
        pltpu.make_async_copy(sent, sent, sem).wait()


def per_device(velocity, elem_scale, face_map, ref_coords, owner_dev, owner_elem):
    deriv = rounded_deriv()
    dtab = np.repeat(deriv.T, 128, axis=1).astype(np.float32)
    vmem = pl.BlockSpec(memory_space=pltpu.VMEM)
    out = pl.pallas_call(
        kernel,
        out_shape=(
            jax.ShapeDtypeStruct((9, 256, 512), BF16),
            jax.ShapeDtypeStruct((12, 1024), F32),
        ),
        in_specs=[pl.BlockSpec(memory_space=pltpu.HBM)] * 12,
        out_specs=(vmem, vmem),
        scratch_shapes=[
            pltpu.VMEM((3, 256, 512), BF16),
            pltpu.VMEM((3, 256), F32),
            pltpu.VMEM((64, 256), jnp.int32),
            pltpu.VMEM((3, 1024), F32),
            pltpu.VMEM((1, 1024), jnp.int32),
            pltpu.VMEM((1, 1024), jnp.int32),
            pltpu.VMEM((512, 256), BF16),
            pltpu.VMEM((512, 512), BF16),
            pltpu.VMEM((256, 512), BF16),
            pltpu.VMEM((256, 256), BF16),
            pltpu.VMEM((128, 256), BF16),
            pltpu.VMEM((8, 1024), F32),
            pltpu.VMEM((3, 256, 128), F32),
            pltpu.VMEM((3, 256, 128), F32),
            pltpu.VMEM((3, 256, 128), F32),
            pltpu.VMEM((3, 256, 128), F32),
            pltpu.VMEM((3, 256), F32),
            pltpu.VMEM((3, 256), F32),
            pltpu.VMEM((128, 128), jnp.int32),
            pltpu.VMEM((128, 128), jnp.int32),
            pltpu.VMEM((128, 1, 128), F32),
            pltpu.VMEM((128, 1, 128), F32),
            pltpu.VMEM((128, 2, 128), F32),
            pltpu.VMEM((128, 2, 128), F32),
            pltpu.VMEM((128, 128), F32),
            pltpu.VMEM((3, 512, 256), BF16),
            pltpu.VMEM((256, 2048), BF16),
            pltpu.VMEM((9, 256, 128), F32),
            pltpu.VMEM((1152, 256), BF16),
            pltpu.VMEM((256, 128), F32),
            pltpu.VMEM((24, 2048), F32),
            pltpu.VMEM((16, 1024), F32),
            pltpu.VMEM((256, 1024), BF16),
            pltpu.VMEM((16, 256), F32),
            pltpu.VMEM((128, 128), F32),
            pltpu.VMEM((128, 128), F32),
            pltpu.SemaphoreType.DMA((14,)),
            pltpu.SemaphoreType.DMA((9,)),
            pltpu.SemaphoreType.DMA((9,)),
            pltpu.SemaphoreType.DMA,
            pltpu.SemaphoreType.DMA,
            pltpu.SemaphoreType.DMA,
            pltpu.SemaphoreType.DMA,
            pltpu.SemaphoreType.REGULAR,
            pltpu.SemaphoreType.REGULAR,
        ],
        compiler_params=pltpu.CompilerParams(
            collective_id=0, has_side_effects=True, vmem_limit_bytes=24 * 1024 * 1024
        ),
    )(
        *(
            pltpu.with_memory_space_constraint(operand, pltpu.HBM)
            for operand in (
                velocity.transpose(1, 0, 2),
                elem_scale.T,
                face_map.T,
                ref_coords,
                owner_dev.reshape(1, 1024),
                owner_elem.reshape(1, 1024),
                *tables(),
                jnp.asarray(dtab),
            )
        )
    )
    return out[0].transpose(1, 0, 2), out[1]


def solution(mesh):
    both = ("group", "member")
    in_specs = (P(both, None, None), P(both, None), P(both, None), P(None, both), P(both, None), P(both))
    out_specs = (P(both, None, None), P(None, both))
    return jax.shard_map(per_device, mesh=mesh, in_specs=in_specs, out_specs=out_specs, check_vma=False)
```

```python
import functools

import jax
import jax.numpy as jnp
import numpy as np
from jax import lax
from jax.experimental import pallas as pl
from jax.experimental.pallas import tpu as pltpu
from jax.sharding import PartitionSpec as P

MESH = pl.DeviceIdType.MESH
F32, BF16 = jnp.float32, jnp.bfloat16
NDEV = 128
EARLY = 1


def gll_nodes():
    return -np.cos(np.pi * np.arange(8) / 7.0)


def deriv_matrix():
    nodes = gll_nodes()
    weights = np.array([np.prod([nodes[a] - nodes[b] for b in range(8) if b != a]) for a in range(8)])
    deriv = np.zeros((8, 8))
    for a in range(8):
        for b in range(8):
            if a != b:
                deriv[a, b] = weights[a] / weights[b] / (nodes[a] - nodes[b])
            else:
                deriv[a, a] = sum(1.0 / (nodes[a] - nodes[o]) for o in range(8) if o != a)
    return deriv


def tables():
    dt = deriv_matrix().astype(np.float32).T
    eye = np.eye(8, dtype=np.float32)
    gr = np.kron(np.kron(dt, eye), eye)
    gs = np.kron(np.kron(eye, dt), eye)
    gt = np.kron(np.kron(eye, eye), dt)
    low = 8 * np.arange(64)
    ident = np.eye(512, dtype=np.float32)
    face = np.concatenate([ident[:, low + 7], gt[:, low + 7], ident[:, low], gt[:, low]], axis=1)
    fr, fs = np.kron(dt, eye), np.kron(eye, dt)
    inner = np.zeros((256, 256), np.float32)
    inner[0:64, 0:64] = fr
    inner[128:192, 64:128] = fr
    inner[0:64, 128:192] = fs
    inner[128:192, 192:256] = fs
    block = np.concatenate([gs[:256, :256], gt[:256, :256]], axis=1)
    upper = np.triu(np.ones((128, 128), np.float32), 1)
    count = np.concatenate([upper, np.ones((128, 128), np.float32)], axis=1)
    return [jnp.asarray(t, BF16) for t in (face, gr, block, inner, count)]


def rounded_deriv():
    return deriv_matrix().astype(np.float32).astype(jnp.dtype(BF16)).astype(np.float32)


def split3(x):
    hi = x.astype(BF16)
    rest = x - hi.astype(F32)
    mid = rest.astype(BF16)
    return hi, mid, (rest - mid.astype(F32)).astype(BF16)


def dot(a, b):
    return jnp.dot(a, b, preferred_element_type=F32)


def dot_t(a, b):
    return lax.dot_general(a, b, (((1,), (1,)), ((), ())), preferred_element_type=F32)


def iota(shape, axis):
    return lax.broadcasted_iota(jnp.int32, shape, axis)


def take_lanes(x, idx):
    return jnp.take_along_axis(x, idx, axis=1, mode="promise_in_bounds")


def column(values):
    row = iota((8, 1), 0)
    out = jnp.full((8, 1), float(values[0]), F32)
    for a in range(1, 8):
        out = jnp.where(row == a, float(values[a]), out)
    return out


def lagrange(y):
    nodes = gll_nodes()
    row = iota(y.shape, 0)
    out = None
    for b in range(8):
        inv = column([1.0 / (nodes[a] - nodes[b]) if a != b else 0.0 for a in range(8)])
        term = jnp.where(row == b, 1.0, (y - float(nodes[b])) * inv)
        out = term if out is None else out * term
    return out


def far_first():
    hops = [0, 1, 2, 1]
    every = [(x, y, z, c) for x in range(4) for y in range(4) for z in range(4) for c in range(2)]
    every.remove((0, 0, 0, 0))
    return sorted(every, key=lambda o: -(hops[o[0]] + hops[o[1]] + hops[o[2]]))


def kernel(v_in, sc_in, fm_in, rc_in, od_in, oe_in, face_in, gr_in, block_in, inner_in, count_in, dtab_in,
           grad, pv,
           v, sc, fm, rc, od, oe, face, gr, block, inner, count, dtab,
           topm, botm, rtop, rbot, scp, scn, invs, invr, sreq, rreq, sret, rret,
           scols, vt, hot, zs, zt, res, wts, rj, hot2, sclanes, rt, fmt,
           ins, hs, hr, qs, qr, ps, pr, sem_a, sem_b):
    loads = {}
    order = [("face", face_in, face), ("v0", v_in.at[0], v.at[0]), ("v1", v_in.at[1], v.at[1]),
             ("v2", v_in.at[2], v.at[2]), ("sc", sc_in, sc), ("od", od_in, od), ("count", count_in, count),
             ("rc", rc_in, rc), ("oe", oe_in, oe), ("fm", fm_in, fm), ("inner", inner_in, inner),
             ("dtab", dtab_in, dtab), ("gr", gr_in, gr), ("block", block_in, block)]
    for k, (name, src, dst) in enumerate(order):
        loads[name] = pltpu.make_async_copy(src, dst, ins.at[k])
        loads[name].start()

    g, m = lax.axis_index("group"), lax.axis_index("member")
    me = g * 16 + m
    core, x, z, y = g % 2, g // 2, m // 4, m % 4
    nxt, prv = (me + 1) % NDEV, (me + NDEV - 1) % NDEV
    nxt, prv = (nxt // 16, nxt % 16), (prv // 16, prv % 16)

    bar = pltpu.get_barrier_semaphore()
    partners = [nxt, prv] + [((g + i) % 8, m) for i in range(1, 8)]
    zpart = [(g, ((z + i) % 4) * 4 + y) for i in range(1, 4)]
    ypart = [(g, z * 4 + (y + i) % 4) for i in range(1, 4)]
    for p in partners + zpart + ypart:
        pl.semaphore_signal(bar, inc=1, device_id=p, device_id_type=MESH)

    loads["face"].wait()
    for c in range(3):
        loads["v%d" % c].wait()
        out = dot(v[c], face[...])
        topm[c] = out[:, :128]
        botm[c] = out[:, 128:]
    loads["sc"].wait()

    loads["fm"].wait()
    fmt[0:64, :] = fm[:, 0:128].astype(F32)
    fmt[64:128, :] = fm[:, 128:256].astype(F32)

    def invert(f, acc):
        lo, hi = acc
        where = iota((64, 128), 0).astype(F32)
        value = f.astype(F32)
        lo = jnp.where(fmt[pl.ds(f, 1), :] == where, value, lo)
        hi = jnp.where(fmt[pl.ds(64 + f, 1), :] == where, value, hi)
        return lo, hi

    zero = jnp.zeros((64, 128), F32)
    inv_lo, inv_hi = lax.fori_loop(0, 64, invert, (zero, zero), unroll=8)
    invs[...] = jnp.concatenate([inv_lo, inv_hi], axis=0).T.astype(jnp.int32)

    pl.semaphore_wait(bar, len(partners) + 6)
    for p in zpart:
        pl.semaphore_signal(sem_a, inc=1, device_id=p, device_id_type=MESH)

    def push(src, dst, k, to):
        copy = pltpu.make_async_remote_copy(
            src_ref=src, dst_ref=dst, send_sem=hs.at[k], recv_sem=hr.at[k], device_id=to, device_id_type=MESH
        )
        copy.start()
        return copy

    halo = {0: push(sc, scp, 0, nxt), 1: push(sc, scn, 1, prv)}

    def push_faces(c):
        halo[2 + 2 * c] = push(topm.at[c], rtop.at[c], 2 + 2 * c, nxt)
        halo[3 + 2 * c] = push(botm.at[c], rbot.at[c], 3 + 2 * c, prv)

    for c in range(EARLY):
        push_faces(c)

    pl.semaphore_wait(sem_a, 3)
    for p in ypart:
        pl.semaphore_signal(sem_b, inc=1, device_id=p, device_id_type=MESH)

    for name in ("od", "count", "rc", "oe"):
        loads[name].wait()
    running = jnp.zeros((128, 128), F32)
    for b in range(8):
        lanes = slice(128 * b, 128 * b + 128)
        hit = (iota((128, 128), 0) == od[:, lanes]).astype(F32)
        hit16 = hit.astype(BF16)
        hot2[0:128, lanes] = hit16
        hot2[128:256, lanes] = hit16
        before = dot(hit16, count[...])
        rank = jnp.sum(hit * (before[:, :128] + running), axis=0, keepdims=True)
        running = running + before[:, 128:]
        rj[:, lanes] = (iota((16, 128), 0).astype(F32) == rank).astype(F32)
    rows = [rc[i : i + 1, :] for i in range(3)] + [oe[...].astype(F32)]
    spread = jnp.concatenate([rj[...] * row for row in rows] + [jnp.zeros((64, 1024), F32)], axis=0)
    send = None
    for part in split3(spread):
        one = dot_t(hot2[0:128, :], part)
        send = one if send is None else send + one
    sreq[:, 0, :] = send

    pl.semaphore_wait(sem_b, 3)

    def exchange(src, dst, ssem, rsem):
        for ox, oy, oz, oc in far_first():
            tg, tm = ((x + ox) % 4) * 2 + (core + oc) % 2, ((z + oz) % 4) * 4 + (y + oy) % 4
            pltpu.make_async_remote_copy(
                src_ref=src.at[tg * 16 + tm], dst_ref=dst.at[me], send_sem=ssem, recv_sem=rsem,
                device_id=(tg, tm), device_id_type=MESH,
            ).start()
        pltpu.make_async_copy(src.at[me], dst.at[me], rsem).start()

    exchange(sreq, rreq, qs, qr)
    halo[8] = push(invs, invr, 8, prv)
    for c in range(EARLY, 3):
        push_faces(c)

    for c in range(3):
        vt[c] = v[c].astype(F32).T.astype(BF16)
    for d in range(3):
        for i, part in enumerate(split3(sc[d : d + 1, :])):
            sclanes[3 * d + i : 3 * d + i + 1, :] = part.astype(F32)
    scales16 = jnp.concatenate([sclanes[0:9, :], jnp.zeros((7, 256), F32)], axis=0).astype(BF16)

    for k in (0, 1, 8):
        halo[k].wait_recv()
    scols[...] = jnp.zeros((128, 128), F32)
    for h in range(2):
        lanes = slice(128 * h, 128 * h + 128)
        scols[8 * h : 8 * h + 3, :] = scp[:, lanes]
        scols[16 + 8 * h : 16 + 8 * h + 3, :] = scn[:, lanes]
        scols[32 + 8 * h : 32 + 8 * h + 3, :] = sc[:, lanes]
    cols = scols[...].T

    def scale_col(base, d):
        first = cols[:, base + d : base + d + 1]
        second = cols[:, base + 8 + d : base + 8 + d + 1]
        return jnp.concatenate([jnp.broadcast_to(first, (128, 128)), jnp.broadcast_to(second, (128, 128))], axis=0)

    left = iota((256, 128), 1) < 64
    both = [jnp.where(left, scale_col(0, d), scale_col(16, d)) for d in range(3)]
    fm2, inv2 = fmt[...].T.astype(jnp.int32), invr[...]
    left2 = iota((128, 128), 1) < 64
    idx = jnp.concatenate(
        [
            jnp.where(left2, fm2, 64 + pltpu.roll(inv2, 64, 1)),
            jnp.where(left2, pltpu.roll(fm2, 64, 1), 64 + inv2),
        ],
        axis=0,
    )
    loads["inner"].wait()
    loads["dtab"].wait()

    def build(c):
        halo[2 + 2 * c].wait_recv()
        halo[3 + 2 * c].wait_recv()
        up, down = rtop[c], rbot[c]
        rs = dot(jnp.concatenate([up, down], axis=1).astype(BF16), inner[...])
        fields = [rs[:, :128], rs[:, 128:], jnp.where(left, pltpu.roll(up, 64, 1), down)]
        for d in range(3):
            turned = take_lanes(fields[d] * both[d], idx)
            zs[3 * c + d] = turned
            zt[384 * c + 128 * d : 384 * c + 128 * d + 128, :] = turned.T.astype(BF16)

    build(0)

    pltpu.make_async_copy(rreq, rreq, qr).wait()
    rt[...] = rreq[:, 0, :].T

    half = column([0.5] + [1.0] * 6 + [0.5])
    dr = [dtab[:, 128 * a : 128 * a + 1] for a in range(8)]

    def pair(row, j):
        return jnp.concatenate([rt[pl.ds(row + 2 * j, 1), :], rt[pl.ds(row + 2 * j + 1, 1), :]], axis=1)

    def put(cc, j, val, add):
        for h in range(2):
            part = val[:, 128 * h : 128 * h + 128]
            row = pl.ds(cc * 16 + 2 * j + h, 1)
            res[row, :] = res[row, :] + part if add else part

    def own(j, carry):
        lanes = pl.ds(pl.multiple_of(j * 256, 256), 256)
        lag, der = [], []
        for a in range(3):
            base = lagrange(jnp.broadcast_to(pair(16 * a, j), (8, 256)))
            wts[8 * a : 8 * a + 8, lanes] = base
            lag.append(base)
            use = base * half if a == 2 else base
            total = None
            for b in range(8):
                term = use[b : b + 1, :] * dr[b]
                total = term if total is None else total + term
            der.append(total)
        hit = (iota((256, 256), 0).astype(F32) == pair(48, j)).astype(F32).astype(BF16)
        hot[:, lanes] = hit
        pieces = dot(scales16, hit)
        ht = lag[2] * half
        for c in range(3):
            picked = dot(vt[c], hit)
            s0 = s1 = s2 = jnp.zeros((8, 256), F32)
            for jj in range(8):
                a0 = a1 = jnp.zeros((8, 256), F32)
                for i in range(8):
                    node = picked[64 * i + 8 * jj : 64 * i + 8 * jj + 8, :]
                    a0 = a0 + lag[0][i : i + 1, :] * node
                    a1 = a1 + der[0][i : i + 1, :] * node
                s0 = s0 + lag[1][jj : jj + 1, :] * a0
                s1 = s1 + der[1][jj : jj + 1, :] * a0
                s2 = s2 + lag[1][jj : jj + 1, :] * a1
            put(c, j, jnp.sum(lag[2] * s0, axis=0, keepdims=True), False)
            for d, part in enumerate((ht * s2, ht * s1, der[2] * s0)):
                scale = pieces[3 * d : 3 * d + 1] + pieces[3 * d + 1 : 3 * d + 2] + pieces[3 * d + 2 : 3 * d + 3]
                put(3 + 3 * c + d, j, jnp.sum(part, axis=0, keepdims=True) * scale, False)
        return carry

    lax.fori_loop(0, 8, own, 0, unroll=8)

    build(1)
    build(2)

    def neighbours(j, carry):
        lanes = pl.ds(pl.multiple_of(j * 256, 256), 256)
        picked = dot(zt[...], hot[:, lanes])
        lr, ls, lt = wts[0:8, lanes], wts[8:16, lanes], wts[16:24, lanes]
        for cd in range(9):
            lo = hi = jnp.zeros((8, 256), F32)
            for i in range(8):
                at = 128 * cd + 8 * i
                lo = lo + lr[i : i + 1, :] * picked[at : at + 8, :]
                hi = hi + lr[i : i + 1, :] * picked[at + 64 : at + 72, :]
            both_faces = 0.5 * (lt[0:1, :] * lo + lt[7:8, :] * hi)
            put(3 + cd, j, jnp.sum(ls * both_faces, axis=0, keepdims=True), True)
        return carry

    lax.fori_loop(0, 8, neighbours, 0, unroll=8)

    res[192:256, :] = jnp.zeros((64, 128), F32)
    sret[:, 0, :] = res[0:128, :].T
    sret[:, 1, :] = res[128:256, :].T
    exchange(sret, rret, ps, pr)

    loads["gr"].wait()
    loads["block"].wait()
    spot = iota((256, 128), 1)
    on_face = (spot % 8 == 0) | (spot % 8 == 7)
    source = spot // 8 + jnp.where(spot % 8 == 7, 64, 0)
    for c in range(3):
        full = [dot(v[c], gr[...])]
        halves = [dot(v[c, :, 256 * h : 256 * h + 256], block[...]) for h in range(2)]
        for d in range(3):
            scale = scale_col(32, d)
            near = zs[3 * c + d]
            for t in range(4):
                lanes = slice(128 * t, 128 * t + 128)
                if d == 0:
                    raw = full[0][:, lanes]
                else:
                    at = 256 * (d - 1) + 128 * (t % 2)
                    raw = halves[t // 2][:, at : at + 128]
                raw = raw * scale
                mean = 0.5 * (raw + take_lanes(near, source + 16 * t))
                grad[3 * c + d, :, lanes] = jnp.where(on_face, mean, raw).astype(BF16)

    pltpu.make_async_copy(rret, rret, pr).wait()
    back = jnp.concatenate([rret[:, 0, :].T, rret[:, 1, :].T[0:64, :]], axis=0)
    hi, lo, _ = split3(back)
    rows = dot(jnp.concatenate([hi, lo], axis=1), hot2[...])
    for cc in range(12):
        pv[cc : cc + 1, :] = jnp.sum(rj[...] * rows[16 * cc : 16 * cc + 16, :], axis=0, keepdims=True)

    for copy in halo.values():
        copy.wait_send()
    for src, sem in ((sreq, qs), (sret, ps)):
        sent = src.at[pl.ds(0, NDEV - 1)]
        pltpu.make_async_copy(sent, sent, sem).wait()


def per_device(velocity, elem_scale, face_map, ref_coords, owner_dev, owner_elem):
    deriv = rounded_deriv()
    dtab = np.repeat(deriv.T, 128, axis=1).astype(np.float32)
    vmem = pl.BlockSpec(memory_space=pltpu.VMEM)
    out = pl.pallas_call(
        kernel,
        out_shape=(
            jax.ShapeDtypeStruct((9, 256, 512), BF16),
            jax.ShapeDtypeStruct((12, 1024), F32),
        ),
        in_specs=[pl.BlockSpec(memory_space=pltpu.HBM)] * 12,
        out_specs=(vmem, vmem),
        scratch_shapes=[
            pltpu.VMEM((3, 256, 512), BF16),
            pltpu.VMEM((3, 256), F32),
            pltpu.VMEM((64, 256), jnp.int32),
            pltpu.VMEM((3, 1024), F32),
            pltpu.VMEM((1, 1024), jnp.int32),
            pltpu.VMEM((1, 1024), jnp.int32),
            pltpu.VMEM((512, 256), BF16),
            pltpu.VMEM((512, 512), BF16),
            pltpu.VMEM((256, 512), BF16),
            pltpu.VMEM((256, 256), BF16),
            pltpu.VMEM((128, 256), BF16),
            pltpu.VMEM((8, 1024), F32),
            pltpu.VMEM((3, 256, 128), F32),
            pltpu.VMEM((3, 256, 128), F32),
            pltpu.VMEM((3, 256, 128), F32),
            pltpu.VMEM((3, 256, 128), F32),
            pltpu.VMEM((3, 256), F32),
            pltpu.VMEM((3, 256), F32),
            pltpu.VMEM((128, 128), jnp.int32),
            pltpu.VMEM((128, 128), jnp.int32),
            pltpu.VMEM((128, 1, 128), F32),
            pltpu.VMEM((128, 1, 128), F32),
            pltpu.VMEM((128, 2, 128), F32),
            pltpu.VMEM((128, 2, 128), F32),
            pltpu.VMEM((128, 128), F32),
            pltpu.VMEM((3, 512, 256), BF16),
            pltpu.VMEM((256, 2048), BF16),
            pltpu.VMEM((9, 256, 128), F32),
            pltpu.VMEM((1152, 256), BF16),
            pltpu.VMEM((256, 128), F32),
            pltpu.VMEM((24, 2048), F32),
            pltpu.VMEM((16, 1024), F32),
            pltpu.VMEM((256, 1024), BF16),
            pltpu.VMEM((16, 256), F32),
            pltpu.VMEM((128, 128), F32),
            pltpu.VMEM((128, 128), F32),
            pltpu.SemaphoreType.DMA((14,)),
            pltpu.SemaphoreType.DMA((9,)),
            pltpu.SemaphoreType.DMA((9,)),
            pltpu.SemaphoreType.DMA,
            pltpu.SemaphoreType.DMA,
            pltpu.SemaphoreType.DMA,
            pltpu.SemaphoreType.DMA,
            pltpu.SemaphoreType.REGULAR,
            pltpu.SemaphoreType.REGULAR,
        ],
        compiler_params=pltpu.CompilerParams(
            collective_id=0, has_side_effects=True, vmem_limit_bytes=24 * 1024 * 1024
        ),
    )(
        *(
            pltpu.with_memory_space_constraint(operand, pltpu.HBM)
            for operand in (
                velocity.transpose(1, 0, 2),
                elem_scale.T,
                face_map.T,
                ref_coords,
                owner_dev.reshape(1, 1024),
                owner_elem.reshape(1, 1024),
                *tables(),
                jnp.asarray(dtab),
            )
        )
    )
    return out[0].transpose(1, 0, 2), out[1]


def solution(mesh):
    both = ("group", "member")
    in_specs = (P(both, None, None), P(both, None), P(both, None), P(None, both), P(both, None), P(both))
    out_specs = (P(both, None, None), P(None, both))
    return jax.shard_map(per_device, mesh=mesh, in_specs=in_specs, out_specs=out_specs, check_vma=False)
```

```python
import functools

import jax
import jax.numpy as jnp
import numpy as np
from jax import lax
from jax.experimental import pallas as pl
from jax.experimental.pallas import tpu as pltpu
from jax.sharding import PartitionSpec as P

MESH = pl.DeviceIdType.MESH
F32, BF16 = jnp.float32, jnp.bfloat16
NDEV = 128
EARLY_TOP, EARLY_BOTTOM = 2, 2


def gll_nodes():
    return -np.cos(np.pi * np.arange(8) / 7.0)


def deriv_matrix():
    nodes = gll_nodes()
    weights = np.array([np.prod([nodes[a] - nodes[b] for b in range(8) if b != a]) for a in range(8)])
    deriv = np.zeros((8, 8))
    for a in range(8):
        for b in range(8):
            if a != b:
                deriv[a, b] = weights[a] / weights[b] / (nodes[a] - nodes[b])
            else:
                deriv[a, a] = sum(1.0 / (nodes[a] - nodes[o]) for o in range(8) if o != a)
    return deriv


def tables():
    dt = deriv_matrix().astype(np.float32).T
    eye = np.eye(8, dtype=np.float32)
    gr = np.kron(np.kron(dt, eye), eye)
    gs = np.kron(np.kron(eye, dt), eye)
    gt = np.kron(np.kron(eye, eye), dt)
    low = 8 * np.arange(64)
    ident = np.eye(512, dtype=np.float32)
    face = np.concatenate([ident[:, low + 7], gt[:, low + 7], ident[:, low], gt[:, low]], axis=1)
    fr, fs = np.kron(dt, eye), np.kron(eye, dt)
    inner = np.zeros((256, 256), np.float32)
    inner[0:64, 0:64] = fr
    inner[128:192, 64:128] = fr
    inner[0:64, 128:192] = fs
    inner[128:192, 192:256] = fs
    block = np.concatenate([gs[:256, :256], gt[:256, :256]], axis=1)
    upper = np.triu(np.ones((128, 128), np.float32), 1)
    count = np.concatenate([upper, np.ones((128, 128), np.float32)], axis=1)
    return [jnp.asarray(t, BF16) for t in (face, gr, block, inner, count)]


def rounded_deriv():
    return deriv_matrix().astype(np.float32).astype(jnp.dtype(BF16)).astype(np.float32)


def split3(x):
    hi = x.astype(BF16)
    rest = x - hi.astype(F32)
    mid = rest.astype(BF16)
    return hi, mid, (rest - mid.astype(F32)).astype(BF16)


def dot(a, b):
    return jnp.dot(a, b, preferred_element_type=F32)


def dot_t(a, b):
    return lax.dot_general(a, b, (((1,), (1,)), ((), ())), preferred_element_type=F32)


def iota(shape, axis):
    return lax.broadcasted_iota(jnp.int32, shape, axis)


def take_lanes(x, idx):
    return jnp.take_along_axis(x, idx, axis=1, mode="promise_in_bounds")


def column(values):
    row = iota((8, 1), 0)
    out = jnp.full((8, 1), float(values[0]), F32)
    for a in range(1, 8):
        out = jnp.where(row == a, float(values[a]), out)
    return out


def lagrange(y):
    nodes = gll_nodes()
    row = iota(y.shape, 0)
    out = None
    for b in range(8):
        inv = column([1.0 / (nodes[a] - nodes[b]) if a != b else 0.0 for a in range(8)])
        term = jnp.where(row == b, 1.0, (y - float(nodes[b])) * inv)
        out = term if out is None else out * term
    return out


def far_first():
    hops = [0, 1, 2, 1]
    every = [(x, y, z, c) for x in range(4) for y in range(4) for z in range(4) for c in range(2)]
    every.remove((0, 0, 0, 0))
    return sorted(every, key=lambda o: -(hops[o[0]] + hops[o[1]] + hops[o[2]]))


def kernel(v_in, sc_in, fm_in, rc_in, od_in, oe_in, face_in, gr_in, block_in, inner_in, count_in, dtab_in,
           grad, back, rj, hot2,
           v, sc, fm, rc, od, oe, face, gr, block, inner, count, dtab,
           topm, botm, rtop, rbot, scp, scn, invs, invr, sreq, rreq, sret, rret,
           scols, vt, hot, zs, zt, res, wts, sclanes, rt, fmt,
           ins, hs, hr, qs, qr, ps, pr, sem_a, sem_b):
    loads = {}
    order = [("face", face_in, face), ("v0", v_in.at[0], v.at[0]), ("v1", v_in.at[1], v.at[1]),
             ("v2", v_in.at[2], v.at[2]), ("sc", sc_in, sc), ("od", od_in, od), ("count", count_in, count),
             ("rc", rc_in, rc), ("oe", oe_in, oe), ("fm", fm_in, fm), ("inner", inner_in, inner),
             ("dtab", dtab_in, dtab), ("gr", gr_in, gr), ("block", block_in, block)]
    for k, (name, src, dst) in enumerate(order):
        loads[name] = pltpu.make_async_copy(src, dst, ins.at[k])
        loads[name].start()

    g, m = lax.axis_index("group"), lax.axis_index("member")
    me = g * 16 + m
    core, x, z, y = g % 2, g // 2, m // 4, m % 4
    nxt, prv = (me + 1) % NDEV, (me + NDEV - 1) % NDEV
    nxt, prv = (nxt // 16, nxt % 16), (prv // 16, prv % 16)

    bar = pltpu.get_barrier_semaphore()
    partners = [nxt, prv] + [((g + i) % 8, m) for i in range(1, 8)]
    zpart = [(g, ((z + i) % 4) * 4 + y) for i in range(1, 4)]
    ypart = [(g, z * 4 + (y + i) % 4) for i in range(1, 4)]
    for p in partners + zpart + ypart:
        pl.semaphore_signal(bar, inc=1, device_id=p, device_id_type=MESH)

    loads["face"].wait()
    for c in range(3):
        loads["v%d" % c].wait()
        out = dot(v[c], face[...])
        topm[c] = out[:, :128]
        botm[c] = out[:, 128:]
    loads["sc"].wait()

    loads["fm"].wait()
    fmt[0:64, :] = fm[:, 0:128].astype(F32)
    fmt[64:128, :] = fm[:, 128:256].astype(F32)

    def invert(f, acc):
        lo, hi = acc
        where = iota((64, 128), 0).astype(F32)
        value = f.astype(F32)
        lo = jnp.where(fmt[pl.ds(f, 1), :] == where, value, lo)
        hi = jnp.where(fmt[pl.ds(64 + f, 1), :] == where, value, hi)
        return lo, hi

    zero = jnp.zeros((64, 128), F32)
    inv_lo, inv_hi = lax.fori_loop(0, 64, invert, (zero, zero), unroll=8)
    invs[...] = jnp.concatenate([inv_lo, inv_hi], axis=0).T.astype(jnp.int32)

    pl.semaphore_wait(bar, len(partners) + 6)
    for p in zpart:
        pl.semaphore_signal(sem_a, inc=1, device_id=p, device_id_type=MESH)

    def push(src, dst, k, to):
        copy = pltpu.make_async_remote_copy(
            src_ref=src, dst_ref=dst, send_sem=hs.at[k], recv_sem=hr.at[k], device_id=to, device_id_type=MESH
        )
        copy.start()
        return copy

    halo = {0: push(sc, scp, 0, nxt), 1: push(sc, scn, 1, prv)}

    def push_top(k):
        c, rows = k // 2, pl.ds(128 * (k % 2), 128)
        halo[3 + k] = push(topm.at[c, rows], rtop.at[c, rows], 3 + k, nxt)

    def push_bottom(k):
        c, rows = k // 2, pl.ds(128 * (k % 2), 128)
        halo[9 + k] = push(botm.at[c, rows], rbot.at[c, rows], 9 + k, prv)

    for k in range(EARLY_TOP):
        push_top(k)
        if k < EARLY_BOTTOM:
            push_bottom(k)
    pl.semaphore_wait(sem_a, 3)
    for p in ypart:
        pl.semaphore_signal(sem_b, inc=1, device_id=p, device_id_type=MESH)

    for name in ("od", "count", "rc", "oe"):
        loads[name].wait()
    running = jnp.zeros((128, 128), F32)
    for b in range(8):
        lanes = slice(128 * b, 128 * b + 128)
        hit = (iota((128, 128), 0) == od[:, lanes]).astype(F32)
        hit16 = hit.astype(BF16)
        hot2[0:128, lanes] = hit16
        hot2[128:256, lanes] = hit16
        before = dot(hit16, count[...])
        rank = jnp.sum(hit * (before[:, :128] + running), axis=0, keepdims=True)
        running = running + before[:, 128:]
        rj[:, lanes] = (iota((16, 128), 0).astype(F32) == rank).astype(F32)
    rows = [rc[i : i + 1, :] for i in range(3)] + [oe[...].astype(F32)]
    spread = jnp.concatenate([rj[...] * row for row in rows] + [jnp.zeros((64, 1024), F32)], axis=0)
    send = None
    for part in split3(spread):
        one = dot_t(hot2[0:128, :], part)
        send = one if send is None else send + one
    sreq[:, 0, :] = send

    pl.semaphore_wait(sem_b, 3)

    def exchange(src, dst, ssem, rsem):
        for ox, oy, oz, oc in far_first():
            tg, tm = ((x + ox) % 4) * 2 + (core + oc) % 2, ((z + oz) % 4) * 4 + (y + oy) % 4
            pltpu.make_async_remote_copy(
                src_ref=src.at[tg * 16 + tm], dst_ref=dst.at[me], send_sem=ssem, recv_sem=rsem,
                device_id=(tg, tm), device_id_type=MESH,
            ).start()
        pltpu.make_async_copy(src.at[me], dst.at[me], rsem).start()

    exchange(sreq, rreq, qs, qr)
    halo[2] = push(invs, invr, 2, prv)
    for k in range(EARLY_BOTTOM, 6):
        push_bottom(k)
        if k >= EARLY_TOP:
            push_top(k)

    for c in range(3):
        vt[c] = v[c].astype(F32).T.astype(BF16)
    for d in range(3):
        for i, part in enumerate(split3(sc[d : d + 1, :])):
            sclanes[3 * d + i : 3 * d + i + 1, :] = part.astype(F32)
    scales16 = jnp.concatenate([sclanes[0:9, :], jnp.zeros((7, 256), F32)], axis=0).astype(BF16)

    for k in (0, 1, 2):
        halo[k].wait_recv()
    scols[...] = jnp.zeros((128, 128), F32)
    for h in range(2):
        lanes = slice(128 * h, 128 * h + 128)
        scols[8 * h : 8 * h + 3, :] = scp[:, lanes]
        scols[16 + 8 * h : 16 + 8 * h + 3, :] = scn[:, lanes]
        scols[32 + 8 * h : 32 + 8 * h + 3, :] = sc[:, lanes]
    cols = scols[...].T

    def scale_col(base, d):
        first = cols[:, base + d : base + d + 1]
        second = cols[:, base + 8 + d : base + 8 + d + 1]
        return jnp.concatenate([jnp.broadcast_to(first, (128, 128)), jnp.broadcast_to(second, (128, 128))], axis=0)

    left = iota((256, 128), 1) < 64
    both = [jnp.where(left, scale_col(0, d), scale_col(16, d)) for d in range(3)]
    fm2, inv2 = fmt[...].T.astype(jnp.int32), invr[...]
    left2 = iota((128, 128), 1) < 64
    idx = jnp.concatenate(
        [
            jnp.where(left2, fm2, 64 + pltpu.roll(inv2, 64, 1)),
            jnp.where(left2, pltpu.roll(fm2, 64, 1), 64 + inv2),
        ],
        axis=0,
    )
    loads["inner"].wait()
    loads["dtab"].wait()

    def build(c):
        for k in (2 * c, 2 * c + 1):
            halo[3 + k].wait_recv()
            halo[9 + k].wait_recv()
        up, down = rtop[c], rbot[c]
        rs = dot(jnp.concatenate([up, down], axis=1).astype(BF16), inner[...])
        fields = [rs[:, :128], rs[:, 128:], jnp.where(left, pltpu.roll(up, 64, 1), down)]
        for d in range(3):
            turned = take_lanes(fields[d] * both[d], idx)
            zs[3 * c + d] = turned
            zt[384 * c + 128 * d : 384 * c + 128 * d + 128, :] = turned.T.astype(BF16)

    build(0)

    pltpu.make_async_copy(rreq, rreq, qr).wait()
    rt[...] = rreq[:, 0, :].T

    half = column([0.5] + [1.0] * 6 + [0.5])
    dr = [dtab[:, 128 * a : 128 * a + 1] for a in range(8)]

    def pair(row, j):
        return jnp.concatenate([rt[pl.ds(row + 2 * j, 1), :], rt[pl.ds(row + 2 * j + 1, 1), :]], axis=1)

    def put(cc, j, val, add):
        for h in range(2):
            part = val[:, 128 * h : 128 * h + 128]
            row = pl.ds(cc * 16 + 2 * j + h, 1)
            res[row, :] = res[row, :] + part if add else part

    def own(j, carry):
        lanes = pl.ds(pl.multiple_of(j * 256, 256), 256)
        lag, der = [], []
        for a in range(3):
            base = lagrange(jnp.broadcast_to(pair(16 * a, j), (8, 256)))
            wts[8 * a : 8 * a + 8, lanes] = base
            lag.append(base)
            use = base * half if a == 2 else base
            total = None
            for b in range(8):
                term = use[b : b + 1, :] * dr[b]
                total = term if total is None else total + term
            der.append(total)
        hit = (iota((256, 256), 0).astype(F32) == pair(48, j)).astype(F32).astype(BF16)
        hot[:, lanes] = hit
        pieces = dot(scales16, hit)
        ht = lag[2] * half
        for c in range(3):
            picked = dot(vt[c], hit)
            s0 = s1 = s2 = jnp.zeros((8, 256), F32)
            for jj in range(8):
                a0 = a1 = jnp.zeros((8, 256), F32)
                for i in range(8):
                    node = picked[64 * i + 8 * jj : 64 * i + 8 * jj + 8, :]
                    a0 = a0 + lag[0][i : i + 1, :] * node
                    a1 = a1 + der[0][i : i + 1, :] * node
                s0 = s0 + lag[1][jj : jj + 1, :] * a0
                s1 = s1 + der[1][jj : jj + 1, :] * a0
                s2 = s2 + lag[1][jj : jj + 1, :] * a1
            put(c, j, jnp.sum(lag[2] * s0, axis=0, keepdims=True), False)
            for d, part in enumerate((ht * s2, ht * s1, der[2] * s0)):
                scale = pieces[3 * d : 3 * d + 1] + pieces[3 * d + 1 : 3 * d + 2] + pieces[3 * d + 2 : 3 * d + 3]
                put(3 + 3 * c + d, j, jnp.sum(part, axis=0, keepdims=True) * scale, False)
        return carry

    lax.fori_loop(0, 8, own, 0, unroll=8)

    def neighbours(first, number):
        def body(j, carry):
            lanes = pl.ds(pl.multiple_of(j * 256, 256), 256)
            picked = dot(zt[384 * first : 384 * (first + number), :], hot[:, lanes])
            lr, ls, lt = wts[0:8, lanes], wts[8:16, lanes], wts[16:24, lanes]
            for cd in range(3 * number):
                lo = hi = jnp.zeros((8, 256), F32)
                for i in range(8):
                    at = 128 * cd + 8 * i
                    lo = lo + lr[i : i + 1, :] * picked[at : at + 8, :]
                    hi = hi + lr[i : i + 1, :] * picked[at + 64 : at + 72, :]
                both_faces = 0.5 * (lt[0:1, :] * lo + lt[7:8, :] * hi)
                put(3 + 3 * first + cd, j, jnp.sum(ls * both_faces, axis=0, keepdims=True), True)
            return carry

        lax.fori_loop(0, 8, body, 0, unroll=8)

    build(1)
    neighbours(0, 2)
    build(2)
    neighbours(2, 1)

    res[192:256, :] = jnp.zeros((64, 128), F32)
    sret[:, 0, :] = res[0:128, :].T
    sret[:, 1, :] = res[128:256, :].T
    exchange(sret, rret, ps, pr)

    loads["gr"].wait()
    loads["block"].wait()
    spot = iota((256, 128), 1)
    on_face = (spot % 8 == 0) | (spot % 8 == 7)
    source = spot // 8 + jnp.where(spot % 8 == 7, 64, 0)
    for c in range(3):
        full = [dot(v[c], gr[...])]
        halves = [dot(v[c, :, 256 * h : 256 * h + 256], block[...]) for h in range(2)]
        for d in range(3):
            scale = scale_col(32, d)
            near = zs[3 * c + d]
            for t in range(4):
                lanes = slice(128 * t, 128 * t + 128)
                if d == 0:
                    raw = full[0][:, lanes]
                else:
                    at = 256 * (d - 1) + 128 * (t % 2)
                    raw = halves[t // 2][:, at : at + 128]
                raw = raw * scale
                mean = 0.5 * (raw + take_lanes(near, source + 16 * t))
                grad[3 * c + d, :, lanes] = jnp.where(on_face, mean, raw).astype(BF16)

    pltpu.make_async_copy(rret, rret, pr).wait()
    back[...] = rret[...]

    for copy in halo.values():
        copy.wait_send()
    for src, sem in ((sreq, qs), (sret, ps)):
        sent = src.at[pl.ds(0, NDEV - 1)]
        pltpu.make_async_copy(sent, sent, sem).wait()


def finish(grad, back, rj, hot2, grad_out, pv, sem):
    copies = [pltpu.make_async_copy(grad.at[k], grad_out.at[k], sem.at[k]) for k in range(9)]
    for copy in copies:
        copy.start()
    table = jnp.concatenate([back[:, 0, :].T, back[:, 1, :].T[0:64, :]], axis=0)
    hi, lo, _ = split3(table)
    rows = dot(jnp.concatenate([hi, lo], axis=1), hot2[...])
    for cc in range(12):
        pv[cc : cc + 1, :] = jnp.sum(rj[...] * rows[16 * cc : 16 * cc + 16, :], axis=0, keepdims=True)
    for copy in copies:
        copy.wait()


def per_device(velocity, elem_scale, face_map, ref_coords, owner_dev, owner_elem):
    deriv = rounded_deriv()
    dtab = np.repeat(deriv.T, 128, axis=1).astype(np.float32)
    vmem = pl.BlockSpec(memory_space=pltpu.VMEM)
    out = pl.pallas_call(
        kernel,
        out_shape=(
            jax.ShapeDtypeStruct((9, 256, 512), BF16),
            jax.ShapeDtypeStruct((128, 2, 128), F32),
            jax.ShapeDtypeStruct((16, 1024), F32),
            jax.ShapeDtypeStruct((256, 1024), BF16),
        ),
        in_specs=[pl.BlockSpec(memory_space=pltpu.HBM)] * 12,
        out_specs=(vmem,) * 4,
        scratch_shapes=[
            pltpu.VMEM((3, 256, 512), BF16),
            pltpu.VMEM((3, 256), F32),
            pltpu.VMEM((64, 256), jnp.int32),
            pltpu.VMEM((3, 1024), F32),
            pltpu.VMEM((1, 1024), jnp.int32),
            pltpu.VMEM((1, 1024), jnp.int32),
            pltpu.VMEM((512, 256), BF16),
            pltpu.VMEM((512, 512), BF16),
            pltpu.VMEM((256, 512), BF16),
            pltpu.VMEM((256, 256), BF16),
            pltpu.VMEM((128, 256), BF16),
            pltpu.VMEM((8, 1024), F32),
            pltpu.VMEM((3, 256, 128), F32),
            pltpu.VMEM((3, 256, 128), F32),
            pltpu.VMEM((3, 256, 128), F32),
            pltpu.VMEM((3, 256, 128), F32),
            pltpu.VMEM((3, 256), F32),
            pltpu.VMEM((3, 256), F32),
            pltpu.VMEM((128, 128), jnp.int32),
            pltpu.VMEM((128, 128), jnp.int32),
            pltpu.VMEM((128, 1, 128), F32),
            pltpu.VMEM((128, 1, 128), F32),
            pltpu.VMEM((128, 2, 128), F32),
            pltpu.VMEM((128, 2, 128), F32),
            pltpu.VMEM((128, 128), F32),
            pltpu.VMEM((3, 512, 256), BF16),
            pltpu.VMEM((256, 2048), BF16),
            pltpu.VMEM((9, 256, 128), F32),
            pltpu.VMEM((1152, 256), BF16),
            pltpu.VMEM((256, 128), F32),
            pltpu.VMEM((24, 2048), F32),
            pltpu.VMEM((16, 256), F32),
            pltpu.VMEM((128, 128), F32),
            pltpu.VMEM((128, 128), F32),
            pltpu.SemaphoreType.DMA((14,)),
            pltpu.SemaphoreType.DMA((15,)),
            pltpu.SemaphoreType.DMA((15,)),
            pltpu.SemaphoreType.DMA,
            pltpu.SemaphoreType.DMA,
            pltpu.SemaphoreType.DMA,
            pltpu.SemaphoreType.DMA,
            pltpu.SemaphoreType.REGULAR,
            pltpu.SemaphoreType.REGULAR,
        ],
        compiler_params=pltpu.CompilerParams(
            collective_id=0, has_side_effects=True, vmem_limit_bytes=24 * 1024 * 1024
        ),
    )(
        *(
            pltpu.with_memory_space_constraint(operand, pltpu.HBM)
            for operand in (
                velocity.transpose(1, 0, 2),
                elem_scale.T,
                face_map.T,
                ref_coords,
                owner_dev.reshape(1, 1024),
                owner_elem.reshape(1, 1024),
                *tables(),
                jnp.asarray(dtab),
            )
        )
    )
    grad, values = pl.pallas_call(
        finish,
        out_shape=(jax.ShapeDtypeStruct((9, 256, 512), BF16), jax.ShapeDtypeStruct((12, 1024), F32)),
        in_specs=[vmem] * 4,
        out_specs=(pl.BlockSpec(memory_space=pltpu.HBM), vmem),
        scratch_shapes=[pltpu.SemaphoreType.DMA((9,))],
        compiler_params=pltpu.CompilerParams(vmem_limit_bytes=16 * 1024 * 1024),
    )(*out)
    return grad.transpose(1, 0, 2), values


def solution(mesh):
    both = ("group", "member")
    in_specs = (P(both, None, None), P(both, None), P(both, None), P(None, both), P(both, None), P(both))
    out_specs = (P(both, None, None), P(None, both))
    return jax.shard_map(per_device, mesh=mesh, in_specs=in_specs, out_specs=out_specs, check_vma=False)
```

```python
import functools

import jax
import jax.numpy as jnp
import numpy as np
from jax import lax
from jax.experimental import pallas as pl
from jax.experimental.pallas import tpu as pltpu
from jax.sharding import PartitionSpec as P

MESH = pl.DeviceIdType.MESH
F32, BF16 = jnp.float32, jnp.bfloat16
NDEV = 128
EARLY_TOP, EARLY_BOTTOM = 2, 2


def gll_nodes():
    return -np.cos(np.pi * np.arange(8) / 7.0)


def deriv_matrix():
    nodes = gll_nodes()
    weights = np.array([np.prod([nodes[a] - nodes[b] for b in range(8) if b != a]) for a in range(8)])
    deriv = np.zeros((8, 8))
    for a in range(8):
        for b in range(8):
            if a != b:
                deriv[a, b] = weights[a] / weights[b] / (nodes[a] - nodes[b])
            else:
                deriv[a, a] = sum(1.0 / (nodes[a] - nodes[o]) for o in range(8) if o != a)
    return deriv


def tables():
    dt = deriv_matrix().astype(np.float32).T
    eye = np.eye(8, dtype=np.float32)
    gr = np.kron(np.kron(dt, eye), eye)
    gs = np.kron(np.kron(eye, dt), eye)
    gt = np.kron(np.kron(eye, eye), dt)
    low = 8 * np.arange(64)
    ident = np.eye(512, dtype=np.float32)
    face = np.concatenate([ident[:, low + 7], gt[:, low + 7], ident[:, low], gt[:, low]], axis=1)
    fr, fs = np.kron(dt, eye), np.kron(eye, dt)
    inner = np.zeros((256, 256), np.float32)
    inner[0:64, 0:64] = fr
    inner[128:192, 64:128] = fr
    inner[0:64, 128:192] = fs
    inner[128:192, 192:256] = fs
    block = np.concatenate([gs[:256, :256], gt[:256, :256]], axis=1)
    upper = np.triu(np.ones((128, 128), np.float32), 1)
    count = np.concatenate([upper, np.ones((128, 128), np.float32)], axis=1)
    return [jnp.asarray(t, BF16) for t in (face, gr, block, inner, count)]


def rounded_deriv():
    return deriv_matrix().astype(np.float32).astype(jnp.dtype(BF16)).astype(np.float32)


def split3(x):
    hi = x.astype(BF16)
    rest = x - hi.astype(F32)
    mid = rest.astype(BF16)
    return hi, mid, (rest - mid.astype(F32)).astype(BF16)


def dot(a, b):
    return jnp.dot(a, b, preferred_element_type=F32)


def dot_t(a, b):
    return lax.dot_general(a, b, (((1,), (1,)), ((), ())), preferred_element_type=F32)


def iota(shape, axis):
    return lax.broadcasted_iota(jnp.int32, shape, axis)


def take_lanes(x, idx):
    return jnp.take_along_axis(x, idx, axis=1, mode="promise_in_bounds")


def column(values):
    row = iota((8, 1), 0)
    out = jnp.full((8, 1), float(values[0]), F32)
    for a in range(1, 8):
        out = jnp.where(row == a, float(values[a]), out)
    return out


def lagrange(y):
    nodes = gll_nodes()
    row = iota(y.shape, 0)
    out = None
    for b in range(8):
        inv = column([1.0 / (nodes[a] - nodes[b]) if a != b else 0.0 for a in range(8)])
        term = jnp.where(row == b, 1.0, (y - float(nodes[b])) * inv)
        out = term if out is None else out * term
    return out


def far_first():
    hops = [0, 1, 2, 1]
    every = [(x, y, z, c) for x in range(4) for y in range(4) for z in range(4) for c in range(2)]
    every.remove((0, 0, 0, 0))
    return sorted(every, key=lambda o: -(hops[o[0]] + hops[o[1]] + hops[o[2]]))


def kernel(v_in, sc_in, fm_in, rc_in, od_in, oe_in, face_in, gr_in, block_in, inner_in, count_in, dtab_in,
           grad, back, rj, hot2,
           v, sc, fm, rc, od, oe, face, gr, block, inner, count, dtab,
           topm, botm, rtop, rbot, scp, scn, invs, invr, sreq, rreq, sret, rret,
           scols, vt, hot, zs, zt, res, wts, sclanes, rt, fmt,
           ins, hs, hr, qs, qr, ps, pr, sem_a, sem_b):
    loads = {}
    order = [("face", face_in, face), ("v0", v_in.at[0], v.at[0]), ("v1", v_in.at[1], v.at[1]),
             ("v2", v_in.at[2], v.at[2]), ("sc", sc_in, sc), ("od", od_in, od), ("count", count_in, count),
             ("rc", rc_in, rc), ("oe", oe_in, oe), ("fm", fm_in, fm), ("inner", inner_in, inner),
             ("dtab", dtab_in, dtab), ("gr", gr_in, gr), ("block", block_in, block)]
    for k, (name, src, dst) in enumerate(order):
        loads[name] = pltpu.make_async_copy(src, dst, ins.at[k])
        loads[name].start()

    g, m = lax.axis_index("group"), lax.axis_index("member")
    me = g * 16 + m
    core, x, z, y = g % 2, g // 2, m // 4, m % 4
    nxt, prv = (me + 1) % NDEV, (me + NDEV - 1) % NDEV
    nxt, prv = (nxt // 16, nxt % 16), (prv // 16, prv % 16)

    bar = pltpu.get_barrier_semaphore()
    partners = [nxt, prv] + [((g + i) % 8, m) for i in range(1, 8)]
    zpart = [(g, ((z + i) % 4) * 4 + y) for i in range(1, 4)]
    ypart = [(g, z * 4 + (y + i) % 4) for i in range(1, 4)]
    for p in partners + zpart + ypart:
        pl.semaphore_signal(bar, inc=1, device_id=p, device_id_type=MESH)

    loads["face"].wait()
    for c in range(3):
        loads["v%d" % c].wait()
        out = dot(v[c], face[...])
        topm[c] = out[:, :128]
        botm[c] = out[:, 128:]
    loads["sc"].wait()

    loads["fm"].wait()
    fmt[0:64, :] = fm[:, 0:128].astype(F32)
    fmt[64:128, :] = fm[:, 128:256].astype(F32)

    def invert(f, acc):
        lo, hi = acc
        where = iota((64, 128), 0).astype(F32)
        value = f.astype(F32)
        lo = jnp.where(fmt[pl.ds(f, 1), :] == where, value, lo)
        hi = jnp.where(fmt[pl.ds(64 + f, 1), :] == where, value, hi)
        return lo, hi

    zero = jnp.zeros((64, 128), F32)
    inv_lo, inv_hi = lax.fori_loop(0, 64, invert, (zero, zero), unroll=8)
    invs[...] = jnp.concatenate([inv_lo, inv_hi], axis=0).T.astype(jnp.int32)

    pl.semaphore_wait(bar, len(partners) + 6)
    for p in zpart:
        pl.semaphore_signal(sem_a, inc=1, device_id=p, device_id_type=MESH)

    def push(src, dst, k, to):
        copy = pltpu.make_async_remote_copy(
            src_ref=src, dst_ref=dst, send_sem=hs.at[k], recv_sem=hr.at[k], device_id=to, device_id_type=MESH
        )
        copy.start()
        return copy

    halo = {0: push(sc, scp, 0, nxt), 1: push(sc, scn, 1, prv)}

    def push_top(k):
        c, rows = k // 2, pl.ds(128 * (k % 2), 128)
        halo[3 + k] = push(topm.at[c, rows], rtop.at[c, rows], 3 + k, nxt)

    def push_bottom(k):
        c, rows = k // 2, pl.ds(128 * (k % 2), 128)
        halo[9 + k] = push(botm.at[c, rows], rbot.at[c, rows], 9 + k, prv)

    for k in range(EARLY_TOP):
        push_top(k)
        if k < EARLY_BOTTOM:
            push_bottom(k)
    pl.semaphore_wait(sem_a, 3)
    for p in ypart:
        pl.semaphore_signal(sem_b, inc=1, device_id=p, device_id_type=MESH)

    for name in ("od", "count", "rc", "oe"):
        loads[name].wait()
    running = jnp.zeros((128, 128), F32)
    for b in range(8):
        lanes = slice(128 * b, 128 * b + 128)
        hit = (iota((128, 128), 0) == od[:, lanes]).astype(F32)
        hit16 = hit.astype(BF16)
        hot2[0:128, lanes] = hit16
        hot2[128:256, lanes] = hit16
        before = dot(hit16, count[...])
        rank = jnp.sum(hit * (before[:, :128] + running), axis=0, keepdims=True)
        running = running + before[:, 128:]
        rj[:, lanes] = (iota((16, 128), 0).astype(F32) == rank).astype(F32)
    rows = [rc[i : i + 1, :] for i in range(3)] + [oe[...].astype(F32)]
    spread = jnp.concatenate([rj[...] * row for row in rows] + [jnp.zeros((64, 1024), F32)], axis=0)
    send = None
    for part in split3(spread):
        one = dot_t(hot2[0:128, :], part)
        send = one if send is None else send + one
    sreq[:, 0, :] = send

    pl.semaphore_wait(sem_b, 3)

    def exchange(src, dst, ssem, rsem):
        for ox, oy, oz, oc in far_first():
            tg, tm = ((x + ox) % 4) * 2 + (core + oc) % 2, ((z + oz) % 4) * 4 + (y + oy) % 4
            pltpu.make_async_remote_copy(
                src_ref=src.at[tg * 16 + tm], dst_ref=dst.at[me], send_sem=ssem, recv_sem=rsem,
                device_id=(tg, tm), device_id_type=MESH,
            ).start()
        pltpu.make_async_copy(src.at[me], dst.at[me], rsem).start()

    exchange(sreq, rreq, qs, qr)
    halo[2] = push(invs, invr, 2, prv)
    for k in range(EARLY_BOTTOM, 6):
        push_bottom(k)
        if k >= EARLY_TOP:
            push_top(k)

    for c in range(3):
        vt[c] = v[c].astype(F32).T.astype(BF16)
    for d in range(3):
        for i, part in enumerate(split3(sc[d : d + 1, :])):
            sclanes[3 * d + i : 3 * d + i + 1, :] = part.astype(F32)
    scales16 = jnp.concatenate([sclanes[0:9, :], jnp.zeros((7, 256), F32)], axis=0).astype(BF16)

    for k in (0, 1, 2):
        halo[k].wait_recv()
    scols[...] = jnp.zeros((128, 128), F32)
    for h in range(2):
        lanes = slice(128 * h, 128 * h + 128)
        scols[8 * h : 8 * h + 3, :] = scp[:, lanes]
        scols[16 + 8 * h : 16 + 8 * h + 3, :] = scn[:, lanes]
        scols[32 + 8 * h : 32 + 8 * h + 3, :] = sc[:, lanes]
    cols = scols[...].T

    def scale_col(base, d):
        first = cols[:, base + d : base + d + 1]
        second = cols[:, base + 8 + d : base + 8 + d + 1]
        return jnp.concatenate([jnp.broadcast_to(first, (128, 128)), jnp.broadcast_to(second, (128, 128))], axis=0)

    left = iota((256, 128), 1) < 64
    both = [jnp.where(left, scale_col(0, d), scale_col(16, d)) for d in range(3)]
    fm2, inv2 = fmt[...].T.astype(jnp.int32), invr[...]
    left2 = iota((128, 128), 1) < 64
    idx = jnp.concatenate(
        [
            jnp.where(left2, fm2, 64 + pltpu.roll(inv2, 64, 1)),
            jnp.where(left2, pltpu.roll(fm2, 64, 1), 64 + inv2),
        ],
        axis=0,
    )
    loads["inner"].wait()
    loads["dtab"].wait()

    def build(c):
        for k in (2 * c, 2 * c + 1):
            halo[3 + k].wait_recv()
            halo[9 + k].wait_recv()
        up, down = rtop[c], rbot[c]
        rs = dot(jnp.concatenate([up, down], axis=1).astype(BF16), inner[...])
        fields = [rs[:, :128], rs[:, 128:], jnp.where(left, pltpu.roll(up, 64, 1), down)]
        for d in range(3):
            turned = take_lanes(fields[d] * both[d], idx)
            zs[3 * c + d] = turned
            zt[384 * c + 128 * d : 384 * c + 128 * d + 128, :] = turned.T.astype(BF16)

    build(0)

    pltpu.make_async_copy(rreq, rreq, qr).wait()
    rt[...] = rreq[:, 0, :].T

    half = column([0.5] + [1.0] * 6 + [0.5])
    dr = [dtab[:, 128 * a : 128 * a + 1] for a in range(8)]

    def pair(row, j):
        return jnp.concatenate([rt[pl.ds(row + 2 * j, 1), :], rt[pl.ds(row + 2 * j + 1, 1), :]], axis=1)

    def put(cc, j, val, add):
        for h in range(2):
            part = val[:, 128 * h : 128 * h + 128]
            row = pl.ds(cc * 16 + 2 * j + h, 1)
            res[row, :] = res[row, :] + part if add else part

    def own(j, carry):
        lanes = pl.ds(pl.multiple_of(j * 256, 256), 256)
        lag, der = [], []
        for a in range(3):
            base = lagrange(jnp.broadcast_to(pair(16 * a, j), (8, 256)))
            wts[8 * a : 8 * a + 8, lanes] = base
            lag.append(base)
            use = base * half if a == 2 else base
            total = None
            for b in range(8):
                term = use[b : b + 1, :] * dr[b]
                total = term if total is None else total + term
            der.append(total)
        hit = (iota((256, 256), 0).astype(F32) == pair(48, j)).astype(F32).astype(BF16)
        hot[:, lanes] = hit
        pieces = dot(scales16, hit)
        ht = lag[2] * half
        for c in range(3):
            picked = dot(vt[c], hit)
            s0 = s1 = s2 = jnp.zeros((8, 256), F32)
            for jj in range(8):
                a0 = a1 = jnp.zeros((8, 256), F32)
                for i in range(8):
                    node = picked[64 * i + 8 * jj : 64 * i + 8 * jj + 8, :]
                    a0 = a0 + lag[0][i : i + 1, :] * node
                    a1 = a1 + der[0][i : i + 1, :] * node
                s0 = s0 + lag[1][jj : jj + 1, :] * a0
                s1 = s1 + der[1][jj : jj + 1, :] * a0
                s2 = s2 + lag[1][jj : jj + 1, :] * a1
            put(c, j, jnp.sum(lag[2] * s0, axis=0, keepdims=True), False)
            for d, part in enumerate((ht * s2, ht * s1, der[2] * s0)):
                scale = pieces[3 * d : 3 * d + 1] + pieces[3 * d + 1 : 3 * d + 2] + pieces[3 * d + 2 : 3 * d + 3]
                put(3 + 3 * c + d, j, jnp.sum(part, axis=0, keepdims=True) * scale, False)
        return carry

    lax.fori_loop(0, 8, own, 0, unroll=8)

    def neighbours(first, number):
        def body(j, carry):
            lanes = pl.ds(pl.multiple_of(j * 256, 256), 256)
            picked = dot(zt[384 * first : 384 * (first + number), :], hot[:, lanes])
            lr, ls, lt = wts[0:8, lanes], wts[8:16, lanes], wts[16:24, lanes]
            for cd in range(3 * number):
                lo = hi = jnp.zeros((8, 256), F32)
                for i in range(8):
                    at = 128 * cd + 8 * i
                    lo = lo + lr[i : i + 1, :] * picked[at : at + 8, :]
                    hi = hi + lr[i : i + 1, :] * picked[at + 64 : at + 72, :]
                both_faces = 0.5 * (lt[0:1, :] * lo + lt[7:8, :] * hi)
                put(3 + 3 * first + cd, j, jnp.sum(ls * both_faces, axis=0, keepdims=True), True)
            return carry

        lax.fori_loop(0, 8, body, 0, unroll=8)

    build(1)
    neighbours(0, 2)
    build(2)
    neighbours(2, 1)

    res[192:256, :] = jnp.zeros((64, 128), F32)
    sret[:, 0, :] = res[0:128, :].T
    sret[:, 1, :] = res[128:256, :].T
    exchange(sret, rret, ps, pr)

    loads["gr"].wait()
    loads["block"].wait()
    spot = iota((256, 128), 1)
    on_face = (spot % 8 == 0) | (spot % 8 == 7)
    source = spot // 8 + jnp.where(spot % 8 == 7, 64, 0)
    for c in range(3):
        full = [dot(v[c], gr[...])]
        halves = [dot(v[c, :, 256 * h : 256 * h + 256], block[...]) for h in range(2)]
        for d in range(3):
            scale = scale_col(32, d)
            near = zs[3 * c + d]
            for t in range(4):
                lanes = slice(128 * t, 128 * t + 128)
                if d == 0:
                    raw = full[0][:, lanes]
                else:
                    at = 256 * (d - 1) + 128 * (t % 2)
                    raw = halves[t // 2][:, at : at + 128]
                raw = raw * scale
                mean = 0.5 * (raw + take_lanes(near, source + 16 * t))
                grad[3 * c + d, :, lanes] = jnp.where(on_face, mean, raw).astype(BF16)

    pltpu.make_async_copy(rret, rret, pr).wait()
    back[...] = rret[...]

    for copy in halo.values():
        copy.wait_send()
    for src, sem in ((sreq, qs), (sret, ps)):
        sent = src.at[pl.ds(0, NDEV - 1)]
        pltpu.make_async_copy(sent, sent, sem).wait()


def finish(grad, back, rj, hot2, grad_out, pv_out, pv, sem):
    copies = [pltpu.make_async_copy(grad.at[k], grad_out.at[k], sem.at[k]) for k in range(9)]
    for copy in copies:
        copy.start()
    table = jnp.concatenate([back[:, 0, :].T, back[:, 1, :].T[0:64, :]], axis=0)
    hi, lo, _ = split3(table)
    rows = dot(jnp.concatenate([hi, lo], axis=1), hot2[...])
    for cc in range(12):
        pv[cc : cc + 1, :] = jnp.sum(rj[...] * rows[16 * cc : 16 * cc + 16, :], axis=0, keepdims=True)
    last = pltpu.make_async_copy(pv, pv_out, sem.at[9])
    last.start()
    for copy in copies + [last]:
        copy.wait()


def per_device(velocity, elem_scale, face_map, ref_coords, owner_dev, owner_elem):
    deriv = rounded_deriv()
    dtab = np.repeat(deriv.T, 128, axis=1).astype(np.float32)
    vmem = pl.BlockSpec(memory_space=pltpu.VMEM)
    out = pl.pallas_call(
        kernel,
        out_shape=(
            jax.ShapeDtypeStruct((9, 256, 512), BF16),
            jax.ShapeDtypeStruct((128, 2, 128), F32),
            jax.ShapeDtypeStruct((16, 1024), F32),
            jax.ShapeDtypeStruct((256, 1024), BF16),
        ),
        in_specs=[pl.BlockSpec(memory_space=pltpu.HBM)] * 12,
        out_specs=(vmem,) * 4,
        scratch_shapes=[
            pltpu.VMEM((3, 256, 512), BF16),
            pltpu.VMEM((3, 256), F32),
            pltpu.VMEM((64, 256), jnp.int32),
            pltpu.VMEM((3, 1024), F32),
            pltpu.VMEM((1, 1024), jnp.int32),
            pltpu.VMEM((1, 1024), jnp.int32),
            pltpu.VMEM((512, 256), BF16),
            pltpu.VMEM((512, 512), BF16),
            pltpu.VMEM((256, 512), BF16),
            pltpu.VMEM((256, 256), BF16),
            pltpu.VMEM((128, 256), BF16),
            pltpu.VMEM((8, 1024), F32),
            pltpu.VMEM((3, 256, 128), F32),
            pltpu.VMEM((3, 256, 128), F32),
            pltpu.VMEM((3, 256, 128), F32),
            pltpu.VMEM((3, 256, 128), F32),
            pltpu.VMEM((3, 256), F32),
            pltpu.VMEM((3, 256), F32),
            pltpu.VMEM((128, 128), jnp.int32),
            pltpu.VMEM((128, 128), jnp.int32),
            pltpu.VMEM((128, 1, 128), F32),
            pltpu.VMEM((128, 1, 128), F32),
            pltpu.VMEM((128, 2, 128), F32),
            pltpu.VMEM((128, 2, 128), F32),
            pltpu.VMEM((128, 128), F32),
            pltpu.VMEM((3, 512, 256), BF16),
            pltpu.VMEM((256, 2048), BF16),
            pltpu.VMEM((9, 256, 128), F32),
            pltpu.VMEM((1152, 256), BF16),
            pltpu.VMEM((256, 128), F32),
            pltpu.VMEM((24, 2048), F32),
            pltpu.VMEM((16, 256), F32),
            pltpu.VMEM((128, 128), F32),
            pltpu.VMEM((128, 128), F32),
            pltpu.SemaphoreType.DMA((14,)),
            pltpu.SemaphoreType.DMA((15,)),
            pltpu.SemaphoreType.DMA((15,)),
            pltpu.SemaphoreType.DMA,
            pltpu.SemaphoreType.DMA,
            pltpu.SemaphoreType.DMA,
            pltpu.SemaphoreType.DMA,
            pltpu.SemaphoreType.REGULAR,
            pltpu.SemaphoreType.REGULAR,
        ],
        compiler_params=pltpu.CompilerParams(
            collective_id=0, has_side_effects=True, vmem_limit_bytes=24 * 1024 * 1024
        ),
    )(
        *(
            pltpu.with_memory_space_constraint(operand, pltpu.HBM)
            for operand in (
                velocity.transpose(1, 0, 2),
                elem_scale.T,
                face_map.T,
                ref_coords,
                owner_dev.reshape(1, 1024),
                owner_elem.reshape(1, 1024),
                *tables(),
                jnp.asarray(dtab),
            )
        )
    )
    grad, values = pl.pallas_call(
        finish,
        out_shape=(jax.ShapeDtypeStruct((9, 256, 512), BF16), jax.ShapeDtypeStruct((12, 1024), F32)),
        in_specs=[vmem] * 4,
        out_specs=(pl.BlockSpec(memory_space=pltpu.HBM),) * 2,
        scratch_shapes=[pltpu.VMEM((12, 1024), F32), pltpu.SemaphoreType.DMA((10,))],
        compiler_params=pltpu.CompilerParams(vmem_limit_bytes=16 * 1024 * 1024),
    )(*out)
    return grad.transpose(1, 0, 2), values


def solution(mesh):
    both = ("group", "member")
    in_specs = (P(both, None, None), P(both, None), P(both, None), P(None, both), P(both, None), P(both))
    out_specs = (P(both, None, None), P(None, both))
    return jax.shard_map(per_device, mesh=mesh, in_specs=in_specs, out_specs=out_specs, check_vma=False)
```

```python
import functools

import jax
import jax.numpy as jnp
import numpy as np
from jax import lax
from jax.experimental import pallas as pl
from jax.experimental.pallas import tpu as pltpu
from jax.sharding import PartitionSpec as P

MESH = pl.DeviceIdType.MESH
F32, BF16 = jnp.float32, jnp.bfloat16
NDEV = 128
EARLY_TOP, EARLY_BOTTOM = 1, 1


def gll_nodes():
    return -np.cos(np.pi * np.arange(8) / 7.0)


def deriv_matrix():
    nodes = gll_nodes()
    weights = np.array([np.prod([nodes[a] - nodes[b] for b in range(8) if b != a]) for a in range(8)])
    deriv = np.zeros((8, 8))
    for a in range(8):
        for b in range(8):
            if a != b:
                deriv[a, b] = weights[a] / weights[b] / (nodes[a] - nodes[b])
            else:
                deriv[a, a] = sum(1.0 / (nodes[a] - nodes[o]) for o in range(8) if o != a)
    return deriv


def tables():
    dt = deriv_matrix().astype(np.float32).T
    eye = np.eye(8, dtype=np.float32)
    gr = np.kron(np.kron(dt, eye), eye)
    gs = np.kron(np.kron(eye, dt), eye)
    gt = np.kron(np.kron(eye, eye), dt)
    low = 8 * np.arange(64)
    ident = np.eye(512, dtype=np.float32)
    face = np.concatenate([ident[:, low + 7], gt[:, low + 7], ident[:, low], gt[:, low]], axis=1)
    fr, fs = np.kron(dt, eye), np.kron(eye, dt)
    inner = np.zeros((256, 256), np.float32)
    inner[0:64, 0:64] = fr
    inner[128:192, 64:128] = fr
    inner[0:64, 128:192] = fs
    inner[128:192, 192:256] = fs
    block = np.concatenate([gs[:256, :256], gt[:256, :256]], axis=1)
    upper = np.triu(np.ones((128, 128), np.float32), 1)
    count = np.concatenate([upper, np.ones((128, 128), np.float32)], axis=1)
    return [jnp.asarray(t, BF16) for t in (face, gr, block, inner, count)]


def rounded_deriv():
    return deriv_matrix().astype(np.float32).astype(jnp.dtype(BF16)).astype(np.float32)


def split3(x):
    hi = x.astype(BF16)
    rest = x - hi.astype(F32)
    mid = rest.astype(BF16)
    return hi, mid, (rest - mid.astype(F32)).astype(BF16)


def dot(a, b):
    return jnp.dot(a, b, preferred_element_type=F32)


def dot_t(a, b):
    return lax.dot_general(a, b, (((1,), (1,)), ((), ())), preferred_element_type=F32)


def iota(shape, axis):
    return lax.broadcasted_iota(jnp.int32, shape, axis)


def take_lanes(x, idx):
    return jnp.take_along_axis(x, idx, axis=1, mode="promise_in_bounds")


def column(values):
    row = iota((8, 1), 0)
    out = jnp.full((8, 1), float(values[0]), F32)
    for a in range(1, 8):
        out = jnp.where(row == a, float(values[a]), out)
    return out


def lagrange(y):
    nodes = gll_nodes()
    row = iota(y.shape, 0)
    out = None
    for b in range(8):
        inv = column([1.0 / (nodes[a] - nodes[b]) if a != b else 0.0 for a in range(8)])
        term = jnp.where(row == b, 1.0, (y - float(nodes[b])) * inv)
        out = term if out is None else out * term
    return out


def far_first():
    hops = [0, 1, 2, 1]
    every = [(x, y, z, c) for x in range(4) for y in range(4) for z in range(4) for c in range(2)]
    every.remove((0, 0, 0, 0))
    return sorted(every, key=lambda o: -(hops[o[0]] + hops[o[1]] + hops[o[2]]))


def kernel(v_in, sc_in, fm_in, rc_in, od_in, oe_in, face_in, gr_in, block_in, inner_in, count_in, dtab_in,
           grad, back, rj, hot2,
           v, sc, fm, rc, od, oe, face, gr, block, inner, count, dtab,
           topm, botm, rtop, rbot, scp, scn, invs, invr, sreq, rreq, sret, rret,
           scols, vt, hot, zs, zt, res, wts, sclanes, rt, fmt,
           ins, hs, hr, qs, qr, ps, pr, sem_a, sem_b):
    loads = {}
    order = [("face", face_in, face), ("v0", v_in.at[0], v.at[0]), ("v1", v_in.at[1], v.at[1]),
             ("v2", v_in.at[2], v.at[2]), ("sc", sc_in, sc), ("od", od_in, od), ("count", count_in, count),
             ("rc", rc_in, rc), ("oe", oe_in, oe), ("fm", fm_in, fm), ("inner", inner_in, inner),
             ("dtab", dtab_in, dtab), ("gr", gr_in, gr), ("block", block_in, block)]
    for k, (name, src, dst) in enumerate(order):
        loads[name] = pltpu.make_async_copy(src, dst, ins.at[k])
        loads[name].start()

    g, m = lax.axis_index("group"), lax.axis_index("member")
    me = g * 16 + m
    core, x, z, y = g % 2, g // 2, m // 4, m % 4
    nxt, prv = (me + 1) % NDEV, (me + NDEV - 1) % NDEV
    nxt, prv = (nxt // 16, nxt % 16), (prv // 16, prv % 16)

    bar = pltpu.get_barrier_semaphore()
    partners = [nxt, prv] + [((g + i) % 8, m) for i in range(1, 8)]
    zpart = [(g, ((z + i) % 4) * 4 + y) for i in range(1, 4)]
    ypart = [(g, z * 4 + (y + i) % 4) for i in range(1, 4)]
    for p in partners + zpart + ypart:
        pl.semaphore_signal(bar, inc=1, device_id=p, device_id_type=MESH)

    loads["face"].wait()
    for c in range(3):
        loads["v%d" % c].wait()
        out = dot(v[c], face[...])
        topm[c] = out[:, :128]
        botm[c] = out[:, 128:]
    loads["sc"].wait()

    loads["fm"].wait()
    fmt[0:64, :] = fm[:, 0:128].astype(F32)
    fmt[64:128, :] = fm[:, 128:256].astype(F32)

    def invert(f, acc):
        lo, hi = acc
        where = iota((64, 128), 0).astype(F32)
        value = f.astype(F32)
        lo = jnp.where(fmt[pl.ds(f, 1), :] == where, value, lo)
        hi = jnp.where(fmt[pl.ds(64 + f, 1), :] == where, value, hi)
        return lo, hi

    zero = jnp.zeros((64, 128), F32)
    inv_lo, inv_hi = lax.fori_loop(0, 64, invert, (zero, zero), unroll=8)
    invs[...] = jnp.concatenate([inv_lo, inv_hi], axis=0).T.astype(jnp.int32)

    pl.semaphore_wait(bar, len(partners) + 6)
    for p in zpart:
        pl.semaphore_signal(sem_a, inc=1, device_id=p, device_id_type=MESH)

    def push(src, dst, k, to):
        copy = pltpu.make_async_remote_copy(
            src_ref=src, dst_ref=dst, send_sem=hs.at[k], recv_sem=hr.at[k], device_id=to, device_id_type=MESH
        )
        copy.start()
        return copy

    halo = {0: push(sc, scp, 0, nxt), 1: push(sc, scn, 1, prv)}

    def push_top(k):
        halo[3 + k] = push(topm.at[k], rtop.at[k], 3 + k, nxt)

    def push_bottom(k):
        halo[6 + k] = push(botm.at[k], rbot.at[k], 6 + k, prv)

    for k in range(EARLY_TOP):
        push_top(k)
        if k < EARLY_BOTTOM:
            push_bottom(k)
    pl.semaphore_wait(sem_a, 3)
    for p in ypart:
        pl.semaphore_signal(sem_b, inc=1, device_id=p, device_id_type=MESH)

    for name in ("od", "count", "rc", "oe"):
        loads[name].wait()
    running = jnp.zeros((128, 128), F32)
    for b in range(8):
        lanes = slice(128 * b, 128 * b + 128)
        hit = (iota((128, 128), 0) == od[:, lanes]).astype(F32)
        hit16 = hit.astype(BF16)
        hot2[0:128, lanes] = hit16
        hot2[128:256, lanes] = hit16
        before = dot(hit16, count[...])
        rank = jnp.sum(hit * (before[:, :128] + running), axis=0, keepdims=True)
        running = running + before[:, 128:]
        rj[:, lanes] = (iota((16, 128), 0).astype(F32) == rank).astype(F32)
    rows = [rc[i : i + 1, :] for i in range(3)] + [oe[...].astype(F32)]
    spread = jnp.concatenate([rj[...] * row for row in rows] + [jnp.zeros((64, 1024), F32)], axis=0)
    send = None
    for part in split3(spread):
        one = dot_t(hot2[0:128, :], part)
        send = one if send is None else send + one
    sreq[:, 0, :] = send

    pl.semaphore_wait(sem_b, 3)

    def exchange(src, dst, ssem, rsem):
        for ox, oy, oz, oc in far_first():
            tg, tm = ((x + ox) % 4) * 2 + (core + oc) % 2, ((z + oz) % 4) * 4 + (y + oy) % 4
            pltpu.make_async_remote_copy(
                src_ref=src.at[tg * 16 + tm], dst_ref=dst.at[me], send_sem=ssem, recv_sem=rsem,
                device_id=(tg, tm), device_id_type=MESH,
            ).start()
        pltpu.make_async_copy(src.at[me], dst.at[me], rsem).start()

    exchange(sreq, rreq, qs, qr)
    halo[2] = push(invs, invr, 2, prv)
    for k in range(EARLY_BOTTOM, 3):
        push_bottom(k)
        if k >= EARLY_TOP:
            push_top(k)

    for c in range(3):
        vt[c] = v[c].astype(F32).T.astype(BF16)
    for d in range(3):
        for i, part in enumerate(split3(sc[d : d + 1, :])):
            sclanes[3 * d + i : 3 * d + i + 1, :] = part.astype(F32)
    scales16 = jnp.concatenate([sclanes[0:9, :], jnp.zeros((7, 256), F32)], axis=0).astype(BF16)

    for k in (0, 1, 2):
        halo[k].wait_recv()
    scols[...] = jnp.zeros((128, 128), F32)
    for h in range(2):
        lanes = slice(128 * h, 128 * h + 128)
        scols[8 * h : 8 * h + 3, :] = scp[:, lanes]
        scols[16 + 8 * h : 16 + 8 * h + 3, :] = scn[:, lanes]
        scols[32 + 8 * h : 32 + 8 * h + 3, :] = sc[:, lanes]
    cols = scols[...].T

    def scale_col(base, d):
        first = cols[:, base + d : base + d + 1]
        second = cols[:, base + 8 + d : base + 8 + d + 1]
        return jnp.concatenate([jnp.broadcast_to(first, (128, 128)), jnp.broadcast_to(second, (128, 128))], axis=0)

    left = iota((256, 128), 1) < 64
    both = [jnp.where(left, scale_col(0, d), scale_col(16, d)) for d in range(3)]
    fm2, inv2 = fmt[...].T.astype(jnp.int32), invr[...]
    left2 = iota((128, 128), 1) < 64
    idx = jnp.concatenate(
        [
            jnp.where(left2, fm2, 64 + pltpu.roll(inv2, 64, 1)),
            jnp.where(left2, pltpu.roll(fm2, 64, 1), 64 + inv2),
        ],
        axis=0,
    )
    loads["inner"].wait()
    loads["dtab"].wait()

    def build(c):
        halo[3 + c].wait_recv()
        halo[6 + c].wait_recv()
        up, down = rtop[c], rbot[c]
        rs = dot(jnp.concatenate([up, down], axis=1).astype(BF16), inner[...])
        fields = [rs[:, :128], rs[:, 128:], jnp.where(left, pltpu.roll(up, 64, 1), down)]
        for d in range(3):
            turned = take_lanes(fields[d] * both[d], idx)
            zs[3 * c + d] = turned
            zt[384 * c + 128 * d : 384 * c + 128 * d + 128, :] = turned.T.astype(BF16)

    build(0)

    pltpu.make_async_copy(rreq, rreq, qr).wait()
    rt[...] = rreq[:, 0, :].T

    half = column([0.5] + [1.0] * 6 + [0.5])
    dr = [dtab[:, 128 * a : 128 * a + 1] for a in range(8)]

    def pair(row, j):
        return jnp.concatenate([rt[pl.ds(row + 2 * j, 1), :], rt[pl.ds(row + 2 * j + 1, 1), :]], axis=1)

    def put(cc, j, val, add):
        for h in range(2):
            part = val[:, 128 * h : 128 * h + 128]
            row = pl.ds(cc * 16 + 2 * j + h, 1)
            res[row, :] = res[row, :] + part if add else part

    def own(j, carry):
        lanes = pl.ds(pl.multiple_of(j * 256, 256), 256)
        lag, der = [], []
        for a in range(3):
            base = lagrange(jnp.broadcast_to(pair(16 * a, j), (8, 256)))
            wts[8 * a : 8 * a + 8, lanes] = base
            lag.append(base)
            use = base * half if a == 2 else base
            total = None
            for b in range(8):
                term = use[b : b + 1, :] * dr[b]
                total = term if total is None else total + term
            der.append(total)
        hit = (iota((256, 256), 0).astype(F32) == pair(48, j)).astype(F32).astype(BF16)
        hot[:, lanes] = hit
        pieces = dot(scales16, hit)
        ht = lag[2] * half
        for c in range(3):
            picked = dot(vt[c], hit)
            s0 = s1 = s2 = jnp.zeros((8, 256), F32)
            for jj in range(8):
                a0 = a1 = jnp.zeros((8, 256), F32)
                for i in range(8):
                    node = picked[64 * i + 8 * jj : 64 * i + 8 * jj + 8, :]
                    a0 = a0 + lag[0][i : i + 1, :] * node
                    a1 = a1 + der[0][i : i + 1, :] * node
                s0 = s0 + lag[1][jj : jj + 1, :] * a0
                s1 = s1 + der[1][jj : jj + 1, :] * a0
                s2 = s2 + lag[1][jj : jj + 1, :] * a1
            put(c, j, jnp.sum(lag[2] * s0, axis=0, keepdims=True), False)
            for d, part in enumerate((ht * s2, ht * s1, der[2] * s0)):
                scale = pieces[3 * d : 3 * d + 1] + pieces[3 * d + 1 : 3 * d + 2] + pieces[3 * d + 2 : 3 * d + 3]
                put(3 + 3 * c + d, j, jnp.sum(part, axis=0, keepdims=True) * scale, False)
        return carry

    lax.fori_loop(0, 8, own, 0, unroll=8)

    def neighbours(first, number):
        def body(j, carry):
            lanes = pl.ds(pl.multiple_of(j * 256, 256), 256)
            picked = dot(zt[384 * first : 384 * (first + number), :], hot[:, lanes])
            lr, ls, lt = wts[0:8, lanes], wts[8:16, lanes], wts[16:24, lanes]
            for cd in range(3 * number):
                lo = hi = jnp.zeros((8, 256), F32)
                for i in range(8):
                    at = 128 * cd + 8 * i
                    lo = lo + lr[i : i + 1, :] * picked[at : at + 8, :]
                    hi = hi + lr[i : i + 1, :] * picked[at + 64 : at + 72, :]
                both_faces = 0.5 * (lt[0:1, :] * lo + lt[7:8, :] * hi)
                put(3 + 3 * first + cd, j, jnp.sum(ls * both_faces, axis=0, keepdims=True), True)
            return carry

        lax.fori_loop(0, 8, body, 0, unroll=8)

    neighbours(0, 1)
    build(1)
    neighbours(1, 1)
    build(2)
    neighbours(2, 1)

    res[192:256, :] = jnp.zeros((64, 128), F32)
    sret[:, 0, :] = res[0:128, :].T
    sret[:, 1, :] = res[128:256, :].T
    exchange(sret, rret, ps, pr)

    loads["gr"].wait()
    loads["block"].wait()
    spot = iota((256, 128), 1)
    on_face = (spot % 8 == 0) | (spot % 8 == 7)
    source = spot // 8 + jnp.where(spot % 8 == 7, 64, 0)
    for c in range(3):
        full = [dot(v[c], gr[...])]
        halves = [dot(v[c, :, 256 * h : 256 * h + 256], block[...]) for h in range(2)]
        for d in range(3):
            scale = scale_col(32, d)
            near = zs[3 * c + d]
            for t in range(4):
                lanes = slice(128 * t, 128 * t + 128)
                if d == 0:
                    raw = full[0][:, lanes]
                else:
                    at = 256 * (d - 1) + 128 * (t % 2)
                    raw = halves[t // 2][:, at : at + 128]
                raw = raw * scale
                mean = 0.5 * (raw + take_lanes(near, source + 16 * t))
                grad[3 * c + d, :, lanes] = jnp.where(on_face, mean, raw).astype(BF16)

    pltpu.make_async_copy(rret, rret, pr).wait()
    back[...] = rret[...]

    for copy in halo.values():
        copy.wait_send()
    for src, sem in ((sreq, qs), (sret, ps)):
        sent = src.at[pl.ds(0, NDEV - 1)]
        pltpu.make_async_copy(sent, sent, sem).wait()


def finish(grad, back, rj, hot2, grad_out, pv_out, pv, sem):
    copies = [pltpu.make_async_copy(grad.at[k], grad_out.at[k], sem.at[k]) for k in range(9)]
    for copy in copies:
        copy.start()
    table = jnp.concatenate([back[:, 0, :].T, back[:, 1, :].T[0:64, :]], axis=0)
    hi, lo, _ = split3(table)
    rows = dot(jnp.concatenate([hi, lo], axis=1), hot2[...])
    for cc in range(12):
        pv[cc : cc + 1, :] = jnp.sum(rj[...] * rows[16 * cc : 16 * cc + 16, :], axis=0, keepdims=True)
    last = pltpu.make_async_copy(pv, pv_out, sem.at[9])
    last.start()
    for copy in copies + [last]:
        copy.wait()


def per_device(velocity, elem_scale, face_map, ref_coords, owner_dev, owner_elem):
    deriv = rounded_deriv()
    dtab = np.repeat(deriv.T, 128, axis=1).astype(np.float32)
    vmem = pl.BlockSpec(memory_space=pltpu.VMEM)
    out = pl.pallas_call(
        kernel,
        out_shape=(
            jax.ShapeDtypeStruct((9, 256, 512), BF16),
            jax.ShapeDtypeStruct((128, 2, 128), F32),
            jax.ShapeDtypeStruct((16, 1024), F32),
            jax.ShapeDtypeStruct((256, 1024), BF16),
        ),
        in_specs=[pl.BlockSpec(memory_space=pltpu.HBM)] * 12,
        out_specs=(vmem,) * 4,
        scratch_shapes=[
            pltpu.VMEM((3, 256, 512), BF16),
            pltpu.VMEM((3, 256), F32),
            pltpu.VMEM((64, 256), jnp.int32),
            pltpu.VMEM((3, 1024), F32),
            pltpu.VMEM((1, 1024), jnp.int32),
            pltpu.VMEM((1, 1024), jnp.int32),
            pltpu.VMEM((512, 256), BF16),
            pltpu.VMEM((512, 512), BF16),
            pltpu.VMEM((256, 512), BF16),
            pltpu.VMEM((256, 256), BF16),
            pltpu.VMEM((128, 256), BF16),
            pltpu.VMEM((8, 1024), F32),
            pltpu.VMEM((3, 256, 128), F32),
            pltpu.VMEM((3, 256, 128), F32),
            pltpu.VMEM((3, 256, 128), F32),
            pltpu.VMEM((3, 256, 128), F32),
            pltpu.VMEM((3, 256), F32),
            pltpu.VMEM((3, 256), F32),
            pltpu.VMEM((128, 128), jnp.int32),
            pltpu.VMEM((128, 128), jnp.int32),
            pltpu.VMEM((128, 1, 128), F32),
            pltpu.VMEM((128, 1, 128), F32),
            pltpu.VMEM((128, 2, 128), F32),
            pltpu.VMEM((128, 2, 128), F32),
            pltpu.VMEM((128, 128), F32),
            pltpu.VMEM((3, 512, 256), BF16),
            pltpu.VMEM((256, 2048), BF16),
            pltpu.VMEM((9, 256, 128), F32),
            pltpu.VMEM((1152, 256), BF16),
            pltpu.VMEM((256, 128), F32),
            pltpu.VMEM((24, 2048), F32),
            pltpu.VMEM((16, 256), F32),
            pltpu.VMEM((128, 128), F32),
            pltpu.VMEM((128, 128), F32),
            pltpu.SemaphoreType.DMA((14,)),
            pltpu.SemaphoreType.DMA((9,)),
            pltpu.SemaphoreType.DMA((9,)),
            pltpu.SemaphoreType.DMA,
            pltpu.SemaphoreType.DMA,
            pltpu.SemaphoreType.DMA,
            pltpu.SemaphoreType.DMA,
            pltpu.SemaphoreType.REGULAR,
            pltpu.SemaphoreType.REGULAR,
        ],
        compiler_params=pltpu.CompilerParams(
            collective_id=0, has_side_effects=True, vmem_limit_bytes=24 * 1024 * 1024
        ),
    )(
        *(
            pltpu.with_memory_space_constraint(operand, pltpu.HBM)
            for operand in (
                velocity.transpose(1, 0, 2),
                elem_scale.T,
                face_map.T,
                ref_coords,
                owner_dev.reshape(1, 1024),
                owner_elem.reshape(1, 1024),
                *tables(),
                jnp.asarray(dtab),
            )
        )
    )
    grad, values = pl.pallas_call(
        finish,
        out_shape=(jax.ShapeDtypeStruct((9, 256, 512), BF16), jax.ShapeDtypeStruct((12, 1024), F32)),
        in_specs=[vmem] * 4,
        out_specs=(pl.BlockSpec(memory_space=pltpu.HBM),) * 2,
        scratch_shapes=[pltpu.VMEM((12, 1024), F32), pltpu.SemaphoreType.DMA((10,))],
        compiler_params=pltpu.CompilerParams(vmem_limit_bytes=16 * 1024 * 1024),
    )(*out)
    return grad.transpose(1, 0, 2), values


def solution(mesh):
    both = ("group", "member")
    in_specs = (P(both, None, None), P(both, None), P(both, None), P(None, both), P(both, None), P(both))
    out_specs = (P(both, None, None), P(None, both))
    return jax.shard_map(per_device, mesh=mesh, in_specs=in_specs, out_specs=out_specs, check_vma=False)
```
